32 devices in a mesh: ty: 4 (over y, x), tx: 8 (over z, core).
Axes of the slice: x: 2, y: 2, z: 4, core: 2. Of those that a mesh axis runs over, the one named last changes fastest.
Arguments:
- transmission: float32 [2, 2, 256, 512], P(None, None, 'ty', 'tx'), may hold values from -4 to 4
- probe_field: float32 [2, 128, 128], replicated, may hold values from -4 to 4
- propagator_phase: float32 [128, 128], replicated, may hold values from -3.140625 to 3.140625
- scan_offsets: int32 [4, 8, 6, 2], P('ty', 'tx'), may hold values from 0 to 64, as said below
- position_counts: int32 [4, 8], P('ty', 'tx'), may hold values from 1 to 6, as said below
- intensities: float32 [4, 8, 6, 128, 128], P('ty', 'tx'), may hold values from 0 to 2
Outputs:
- updated_object: float32 [2, 2, 256, 512], P(None, None, 'ty', 'tx')
The draws below stay inside these ranges and needn't reach their ends.
Inputs may be any that keep to these rules, and one draw needn't show every extreme that they name: `scan_offsets`: each pair is a row and a column offset within the extended region of 192 pixels; offsets 0 and 64 both occur. `position_counts`: positions k of a tile with k >= its count are ignored; some tile has 6 and some tile has 1.
All inputs are finite; a program needn't handle non-finite values.
Results may differ from the reference program's by a relative error of at most 0.0003.
Values sent between devices are 32-bit elements; how exact they have to be, the bound alone decides.
No kernel may reach another device: no remote copies, remote signals or barrier semaphores. Data moves between devices by JAX's collectives and lax.ppermute only.
A program may use at most 64 MiB of HBM per device.

```python
import jax
import jax.numpy as jnp
from jax import lax

PROBE = 128
SLICES = 2
KPOS = 6
ITERS = 2
TY_TILES = 4
TX_TILES = 8
NY = 256
NX = 512


def draw_scan_offsets(key, part):
    base = jax.random.randint(key, (TY_TILES, TX_TILES, KPOS, 2), 0, PROBE // 2 + 1)
    base = base.at[0, 0, 0, 0].set(PROBE // 2)
    base = base.at[0, 0, 1, 1].set(0)
    return base.astype(jnp.int32)


def draw_position_counts(key, part):
    total = TY_TILES * TX_TILES
    flat = jax.random.randint(jax.random.fold_in(key, 11), (total,), 1, KPOS + 1)
    chosen = jax.random.randint(jax.random.fold_in(key, 12), (), 0, total)
    index = jnp.arange(total, dtype=jnp.int32)
    flat = jnp.where(index == chosen, KPOS, flat)
    flat = jnp.where(index == (chosen + 1) % total, 1, flat)
    return flat.reshape(TY_TILES, TX_TILES).astype(jnp.int32)


def block_scale(rng, dims, pieces, smallest, high):
    level, own = 1.0, jax.random.fold_in(rng, 6)
    for dim, shards_of in pieces:
        draws = jnp.exp(jax.random.uniform(jax.random.fold_in(own, dim), (shards_of,), jnp.float32, smallest / len(pieces), high / len(pieces)))
        level = level * jnp.repeat(draws, dims[dim] // shards_of).reshape([-1 if axis == dim else 1 for axis in range(len(dims))])
    return level


def scatter_about(stream_key, dims, scale, bound, split=(), held_as=jnp.bfloat16):
    result = jax.random.normal(stream_key, dims, jnp.float32) * scale
    if len(split) > 0:
        result = block_scale(stream_key, dims, split, -0.22, 0.18) * result
    return jnp.clip(result, min=-bound, max=bound).astype(held_as)


def setup_inputs(seed: int = 0) -> dict:
    streams_of = jax.random.split(jax.random.key(seed), 7)
    return {
        "transmission": scatter_about(streams_of[0], (2, SLICES, NY, NX), 0.7, 4.0, ((2, 4), (3, 8)), jnp.float32),
        "probe_field": scatter_about(streams_of[1], (2, PROBE, PROBE), 0.7, 4.0, (), jnp.float32),
        "propagator_phase": jnp.clip(jax.random.uniform(streams_of[2], (PROBE, PROBE), jnp.float32, -3.140625, 3.140625), -3.140625, 3.140625),
        "scan_offsets": draw_scan_offsets(jax.random.fold_in(streams_of[6], 71), 0),
        "position_counts": draw_position_counts(jax.random.fold_in(streams_of[6], 71), 0),
        "intensities": jnp.clip(2.0 * jax.random.uniform(streams_of[5], (TY_TILES, TX_TILES, KPOS, PROBE, PROBE), jnp.float32) ** block_scale(streams_of[5], (TY_TILES, TX_TILES, KPOS, PROBE, PROBE), ((0, 4), (1, 8)), -0.2, 0.2), 0.0, 2.0),
    }


def tile_loss(extended, probe_field, propagator, offsets, active, measured):
    size = probe_field.shape[1]
    layers = extended.shape[1]
    zero_index = jnp.zeros((), jnp.int32)

    def window(offset):
        return lax.dynamic_slice(extended, (zero_index, zero_index, offset[0].astype(jnp.int32), offset[1].astype(jnp.int32)), (2, layers, size, size))
    windows = jax.vmap(window)(offsets)
    field = (probe_field[0] + 1j * probe_field[1])[None]
    for layer in range(layers):
        slice_field = windows[:, 0, layer] + 1j * windows[:, 1, layer]
        field = field * slice_field
        if layer < layers - 1:
            field = jnp.fft.ifft2(propagator[None] * jnp.fft.fft2(field, norm='ortho'), norm='ortho')
    far_field = jnp.fft.fft2(field, norm='ortho')
    power = jnp.real(far_field) ** 2 + jnp.imag(far_field) ** 2
    return jnp.sum(active[:, None, None] * (power - measured) ** 2)

def reference(transmission, probe_field, propagator_phase, scan_offsets, position_counts, intensities):
    core = PROBE // 2
    layers = transmission.shape[1]
    propagator = jnp.cos(propagator_phase) + 1j * jnp.sin(propagator_phase)
    slots = jnp.arange(KPOS, dtype=jnp.int32)
    tiles = jnp.arange(TY_TILES * TX_TILES, dtype=jnp.int32)
    zero_index = jnp.zeros((), jnp.int32)
    current = transmission
    for sweep in range(ITERS):
        padded = jnp.pad(current, ((0, 0), (0, 0), (core, core), (core, core)))

        def visit(total, tile):
            row_index = (tile // TX_TILES).astype(jnp.int32)
            col_index = (tile % TX_TILES).astype(jnp.int32)
            start = (zero_index, zero_index, row_index * core, col_index * core)
            extended = lax.dynamic_slice(padded, start, (2, layers, 3 * core, 3 * core))
            active = (slots < position_counts[row_index, col_index]).astype(jnp.float32)
            grad_tile = jax.grad(tile_loss)(extended, probe_field, propagator, scan_offsets[row_index, col_index], active, intensities[row_index, col_index])
            region = lax.dynamic_slice(total, start, (2, layers, 3 * core, 3 * core))
            return (lax.dynamic_update_slice(total, region + grad_tile, start), None)
        summed, unused = lax.scan(visit, jnp.zeros(padded.shape, jnp.float32), tiles)
        current = current - 0.003 * summed[:, :, core:-core, core:-core]
    return current
```

```python
import math

import jax
import jax.numpy as jnp
import numpy as np
from jax import lax
from jax.experimental import pallas as pl
from jax.experimental.pallas import tpu as pltpu
from jax.sharding import PartitionSpec as P

ITERS = 2
STEP = 0.003
GROUP = 2


def dft_blocks(length):
    index = np.arange(length)
    angle = 2.0 * math.pi / length * (index[:, None] * index[None, :] % length)
    re, im = np.cos(angle) / math.sqrt(length), -np.sin(angle) / math.sqrt(length)
    full = np.block([[re, -im], [im, re]])
    high = full.astype(jnp.bfloat16)
    low = (full - high.astype(np.float64)).astype(jnp.bfloat16)
    return np.stack([high, low, high.T, low.T])


def halves(x):
    high = x.astype(jnp.bfloat16)
    return high, (x - high.astype(jnp.float32)).astype(jnp.bfloat16)


def mm(a, b):
    return jnp.dot(a, b, preferred_element_type=jnp.float32)


def gradient_kernel(
    offsets, count, place, far_ref, mid_ref, near_ref, probe_ref, prop_ref, data_ref, table_ref,
    gfar_ref, gmid_ref, gnear_ref, ext, acc,
):
    layers, rows, lanes = mid_ref.shape
    length = probe_ref.shape[1]
    core = lanes // 2
    lane = lax.broadcasted_iota(jnp.int32, (rows, lanes), 1)
    low_half = lane < core
    is_first, has_far = place[0] == 1, place[1] == 1
    for s in range(layers):
        outer = jnp.where(has_far, far_ref[s], 0.0)
        left = jnp.where(is_first, outer, near_ref[s])
        right = jnp.where(is_first, near_ref[s], outer)
        mid = mid_ref[s]
        ext[s, 0, 0] = jnp.where(low_half, left, pltpu.roll(mid, core, 1))
        ext[s, 1, 0] = jnp.where(low_half, pltpu.roll(left, core, 1), mid)
        ext[s, 0, 1] = right
        ext[s, 1, 1] = pltpu.roll(right, core, 1)
    acc[...] = jnp.zeros_like(acc)

    def right_mul(blocks, table):
        x = jnp.concatenate([jnp.concatenate([r, i], axis=1) for r, i in blocks], axis=0)
        xh, xl = halves(x)
        th, tl = table_ref[2 * table], table_ref[2 * table + 1]
        y = mm(xh, th) + (mm(xl, th) + mm(xh, tl))
        return [
            (y[q * length : (q + 1) * length, :length], y[q * length : (q + 1) * length, length:])
            for q in range(len(blocks))
        ]

    def left_mul(blocks, table):
        x = jnp.concatenate(
            [
                jnp.concatenate([r for r, _ in blocks], axis=1),
                jnp.concatenate([i for _, i in blocks], axis=1),
            ],
            axis=0,
        )
        xh, xl = halves(x)
        th, tl = table_ref[2 * table], table_ref[2 * table + 1]
        y = mm(th, xh) + (mm(th, xl) + mm(tl, xh))
        return [
            (y[:length, q * length : (q + 1) * length], y[length:, q * length : (q + 1) * length])
            for q in range(len(blocks))
        ]

    def fourier(blocks):
        return left_mul(right_mul(blocks, 1), 0)

    def inverse(blocks):
        return left_mul(right_mul(blocks, 0), 1)

    def times(a, b):
        return a[0] * b[0] - a[1] * b[1], a[0] * b[1] + a[1] * b[0]

    def conj_times(a, b):
        return a[0] * b[0] + a[1] * b[1], a[0] * b[1] - a[1] * b[0]

    wide = lax.broadcasted_iota(jnp.int32, (length, lanes), 1)

    @pl.loop(0, pl.cdiv(count[0], GROUP))
    def _(trip):
        slots = [jnp.minimum(trip * GROUP + q, offsets.shape[0] // 2 - 1) for q in range(GROUP)]
        weight = [
            jnp.where(trip * GROUP + q < count[0], 4.0, 0.0).astype(jnp.float32)
            for q in range(GROUP)
        ]
        row = [offsets[2 * k] for k in slots]
        col = [offsets[2 * k + 1] for k in slots]

        def window(q, s):
            back = jnp.where(col[q] == 0, 0, lanes - col[q])
            parts = []
            for part in range(2):
                near = pltpu.roll(ext[s, part, 0, pl.ds(row[q], length), :], back, 1)
                far = pltpu.roll(ext[s, part, 1, pl.ds(row[q], length), :], back, 1)
                parts.append(jnp.where(wide < lanes - col[q], near, far))
            return tuple(parts)

        prop = (prop_ref[0], prop_ref[1])
        probe = (probe_ref[0], probe_ref[1])
        fields = [[probe] * GROUP]
        for s in range(layers):
            exits = [times(fields[s][q], window(q, s)) for q in range(GROUP)]
            if s < layers - 1:
                spectrum = [times(b, prop) for b in fourier(exits)]
                fields.append(inverse(spectrum))
        far = fourier(exits)
        back = []
        for q in range(GROUP):
            re, im = far[q]
            factor = weight[q] * (re * re + im * im - data_ref[slots[q]])
            back.append((factor * re, factor * im))
        grad = inverse(back)
        for s in reversed(range(layers)):
            for q in range(GROUP):
                own = conj_times(fields[s][q], grad[q])
                for part in range(2):
                    turned = pltpu.roll(own[part], col[q], 1)
                    rows_of = pl.ds(row[q], length)
                    acc[s, part, 0, rows_of, :] += jnp.where(wide >= col[q], turned, 0.0)
                    acc[s, part, 1, rows_of, :] += jnp.where(wide < col[q], turned, 0.0)
            if s > 0:
                spectrum = fourier([conj_times(window(q, s), grad[q]) for q in range(GROUP)])
                grad = inverse([conj_times(prop, b) for b in spectrum])

    for s in range(layers):
        re0, re1, im0, im1 = acc[s, 0, 0], acc[s, 0, 1], acc[s, 1, 0], acc[s, 1, 1]
        left = jnp.where(low_half, re0, pltpu.roll(im0, core, 1))
        right = jnp.where(low_half, re1, pltpu.roll(im1, core, 1))
        gmid_ref[s] = jnp.where(low_half, pltpu.roll(re0, core, 1), im0)
        gfar_ref[s] = jnp.where(is_first, left, right)
        gnear_ref[s] = jnp.where(is_first, right, left)


def tile_gradient(offsets, count, place, far, mid, near, probe, prop, data, table):
    layers, rows, lanes = mid.shape
    vmem = pl.BlockSpec(memory_space=pltpu.VMEM)
    smem = pl.BlockSpec(memory_space=pltpu.SMEM)
    strip = jax.ShapeDtypeStruct(mid.shape, jnp.float32)
    return pl.pallas_call(
        gradient_kernel,
        out_shape=(strip, strip, strip),
        in_specs=[smem] * 3 + [vmem] * 7,
        out_specs=(vmem, vmem, vmem),
        scratch_shapes=[pltpu.VMEM((layers, 2, 2, rows, lanes), jnp.float32)] * 2,
        compiler_params=pltpu.CompilerParams(vmem_limit_bytes=32 * 1024 * 1024),
        name="tile_gradient",
    )(offsets, count, place, far, mid, near, probe, prop, data, table)


def around(shard, axis, by):
    count = lax.axis_size(axis)
    return lax.ppermute(shard, axis, [(i, (i + by) % count) for i in range(count)])


def partners(far, near, axis):
    count = lax.axis_size(axis)
    ends = count - 1
    outer = [(i, min(max(i + 1 if i % 2 else i - 1, 0), ends)) for i in range(count)]
    inner = [(i, i ^ 1) for i in range(count)]
    return lax.ppermute(far, axis, outer), lax.ppermute(near, axis, inner)


def on_device(
    transmission, probe_field, propagator_phase, scan_offsets, position_counts, intensities
):
    core = transmission.shape[2]
    tall, broad = lax.axis_size("ty"), lax.axis_size("tx")
    row, col = lax.axis_index("ty"), lax.axis_index("tx")
    table = jnp.asarray(dft_blocks(probe_field.shape[1]))
    prop = jnp.stack([jnp.cos(propagator_phase), jnp.sin(propagator_phase)])
    is_first = col % 2 == 0
    has_far = jnp.where(is_first, col > 0, col < broad - 1)
    place = jnp.stack([is_first, has_far]).astype(jnp.int32)
    has_above, has_below = row > 0, row < tall - 1

    def gradient(strip, far, near):
        gfar, gmid, gnear = tile_gradient(
            scan_offsets.reshape(-1), position_counts.reshape(-1), place, far, strip, near,
            probe_field, prop, intensities[0, 0], table,
        )
        far, near = partners(gfar, gnear, "tx")
        return gmid + near + jnp.where(has_far, far, 0.0)

    own = jnp.concatenate([transmission[0], transmission[1]], axis=-1)
    above = jnp.where(has_above, around(own, "ty", 1), 0.0)
    below = jnp.where(has_below, around(own, "ty", -1), 0.0)
    strip = jnp.concatenate([above, own, below], axis=1)
    for sweep in range(ITERS):
        total = gradient(strip, *partners(strip, strip, "tx"))
        top, mid, bottom = total[:, :core], total[:, core : 2 * core], total[:, 2 * core :]
        if sweep < ITERS - 1:
            down = jnp.where(has_above, around(total[:, core:], "ty", 1), 0.0)
            up = jnp.where(has_below, around(total[:, : 2 * core], "ty", -1), 0.0)
            if tall == 4:
                mixed = around(jnp.where(row < 2, bottom, top), "ty", 2)
                down2, up2 = jnp.where(row < 2, 0.0, mixed), jnp.where(row < 2, mixed, 0.0)
            else:
                down2 = jnp.where(row > 1, around(bottom, "ty", 2), 0.0)
                up2 = jnp.where(row < tall - 2, around(top, "ty", -2), 0.0)
            above = jnp.where(has_above, top + down[:, :core] + down2, 0.0)
            inside = mid + down[:, core:] + up[:, :core]
            below = jnp.where(has_below, bottom + up[:, core:] + up2, 0.0)
            strip = strip - STEP * jnp.concatenate([above, inside, below], axis=1)
        else:
            down = jnp.where(has_above, around(bottom, "ty", 1), 0.0)
            up = jnp.where(has_below, around(top, "ty", -1), 0.0)
            own = strip[:, core : 2 * core] - STEP * (mid + down + up)
    return jnp.stack([own[..., :core], own[..., core:]])


def solution(mesh):
    in_specs = (
        P(None, None, "ty", "tx"),
        P(),
        P(),
        P("ty", "tx", None, None),
        P("ty", "tx"),
        P("ty", "tx", None, None, None),
    )
    return jax.shard_map(
        on_device, mesh=mesh, in_specs=in_specs, out_specs=P(None, None, "ty", "tx"), check_vma=False
    )
```

```python
import math

import jax
import jax.numpy as jnp
import numpy as np
from jax import lax
from jax.experimental import pallas as pl
from jax.experimental.pallas import tpu as pltpu
from jax.sharding import PartitionSpec as P

ITERS = 2
STEP = 0.003
GROUP = 6


def dft_blocks(length):
    index = np.arange(length)
    angle = 2.0 * math.pi / length * (index[:, None] * index[None, :] % length)
    re, im = np.cos(angle) / math.sqrt(length), -np.sin(angle) / math.sqrt(length)
    full = np.block([[re, -im], [im, re]])
    high = full.astype(jnp.bfloat16)
    low = (full - high.astype(np.float64)).astype(jnp.bfloat16)
    return np.stack([high, low, high.T, low.T])


def halves(x):
    high = x.astype(jnp.bfloat16)
    return high, (x - high.astype(jnp.float32)).astype(jnp.bfloat16)


def mm(a, b):
    return jnp.dot(a, b, preferred_element_type=jnp.float32)


def gradient_kernel(
    offsets, count, place, far_ref, mid_ref, near_ref, probe_ref, prop_ref, data_ref, table_ref,
    gfar_ref, gmid_ref, gnear_ref, ext, acc,
):
    layers, rows, lanes = mid_ref.shape
    length = probe_ref.shape[1]
    core = lanes // 2
    positions = offsets.shape[0] // 2
    group = min(GROUP, positions)
    lane = lax.broadcasted_iota(jnp.int32, (rows, lanes), 1)
    low_half = lane < core
    is_first, has_far = place[0] == 1, place[1] == 1
    for s in range(layers):
        outer = jnp.where(has_far, far_ref[s], 0.0)
        left = jnp.where(is_first, outer, near_ref[s])
        right = jnp.where(is_first, near_ref[s], outer)
        mid = mid_ref[s]
        ext[s, 0, 0] = jnp.where(low_half, left, pltpu.roll(mid, core, 1))
        ext[s, 1, 0] = jnp.where(low_half, pltpu.roll(left, core, 1), mid)
        ext[s, 0, 1] = right
        ext[s, 1, 1] = pltpu.roll(right, core, 1)
    acc[...] = jnp.zeros_like(acc)

    def right_mul(blocks, table):
        x = jnp.concatenate([jnp.concatenate([r, i], axis=1) for r, i in blocks], axis=0)
        xh, xl = halves(x)
        th, tl = table_ref[2 * table], table_ref[2 * table + 1]
        y = mm(xh, th) + (mm(xl, th) + mm(xh, tl))
        return [
            (y[q * length : (q + 1) * length, :length], y[q * length : (q + 1) * length, length:])
            for q in range(len(blocks))
        ]

    def left_mul(blocks, table):
        x = jnp.concatenate(
            [
                jnp.concatenate([r for r, _ in blocks], axis=1),
                jnp.concatenate([i for _, i in blocks], axis=1),
            ],
            axis=0,
        )
        xh, xl = halves(x)
        th, tl = table_ref[2 * table], table_ref[2 * table + 1]
        y = mm(th, xh) + (mm(th, xl) + mm(tl, xh))
        return [
            (y[:length, q * length : (q + 1) * length], y[length:, q * length : (q + 1) * length])
            for q in range(len(blocks))
        ]

    def fourier(blocks):
        return left_mul(right_mul(blocks, 1), 0)

    def inverse(blocks):
        return left_mul(right_mul(blocks, 0), 1)

    def times(a, b):
        return a[0] * b[0] - a[1] * b[1], a[0] * b[1] + a[1] * b[0]

    def conj_times(a, b):
        return a[0] * b[0] + a[1] * b[1], a[0] * b[1] - a[1] * b[0]

    wide = lax.broadcasted_iota(jnp.int32, (length, lanes), 1)

    @pl.loop(0, pl.cdiv(count[0], group))
    def _(trip):
        slots = [jnp.minimum(trip * group + q, positions - 1) for q in range(group)]
        weight = [
            jnp.where(trip * group + q < count[0], 4.0, 0.0).astype(jnp.float32)
            for q in range(group)
        ]
        row = [offsets[2 * k] for k in slots]
        col = [offsets[2 * k + 1] for k in slots]

        def window(q, s):
            back = jnp.where(col[q] == 0, 0, lanes - col[q])
            parts = []
            for part in range(2):
                rows_of = pl.ds(row[q], length)
                both = jnp.where(wide >= col[q], ext[s, part, 0, rows_of, :], ext[s, part, 1, rows_of, :])
                parts.append(pltpu.roll(both, back, 1))
            return tuple(parts)

        prop = (prop_ref[0], prop_ref[1])
        probe = (probe_ref[0], probe_ref[1])
        windows = [[window(q, s) for q in range(group)] for s in range(layers)]
        fields = [[probe] * group]
        for s in range(layers):
            exits = [times(fields[s][q], windows[s][q]) for q in range(group)]
            if s < layers - 1:
                spectrum = [times(b, prop) for b in fourier(exits)]
                fields.append(inverse(spectrum))
        far = fourier(exits)
        back = []
        for q in range(group):
            re, im = far[q]
            factor = weight[q] * (re * re + im * im - data_ref[slots[q]])
            back.append((factor * re, factor * im))
        grad = inverse(back)
        for s in reversed(range(layers)):
            for q in range(group):
                own = conj_times(fields[s][q], grad[q])
                for part in range(2):
                    turned = pltpu.roll(own[part], col[q], 1)
                    rows_of = pl.ds(row[q], length)
                    acc[s, part, 0, rows_of, :] += jnp.where(wide >= col[q], turned, 0.0)
                    acc[s, part, 1, rows_of, :] += jnp.where(wide < col[q], turned, 0.0)
            if s > 0:
                spectrum = fourier([conj_times(windows[s][q], grad[q]) for q in range(group)])
                grad = inverse([conj_times(prop, b) for b in spectrum])

    for s in range(layers):
        re0, re1, im0, im1 = acc[s, 0, 0], acc[s, 0, 1], acc[s, 1, 0], acc[s, 1, 1]
        left = jnp.where(low_half, re0, pltpu.roll(im0, core, 1))
        right = jnp.where(low_half, re1, pltpu.roll(im1, core, 1))
        gmid_ref[s] = jnp.where(low_half, pltpu.roll(re0, core, 1), im0)
        gfar_ref[s] = jnp.where(is_first, left, right)
        gnear_ref[s] = jnp.where(is_first, right, left)


def tile_gradient(offsets, count, place, far, mid, near, probe, prop, data, table):
    layers, rows, lanes = mid.shape
    vmem = pl.BlockSpec(memory_space=pltpu.VMEM)
    smem = pl.BlockSpec(memory_space=pltpu.SMEM)
    strip = jax.ShapeDtypeStruct(mid.shape, jnp.float32)
    return pl.pallas_call(
        gradient_kernel,
        out_shape=(strip, strip, strip),
        in_specs=[smem] * 3 + [vmem] * 7,
        out_specs=(vmem, vmem, vmem),
        scratch_shapes=[pltpu.VMEM((layers, 2, 2, rows, lanes), jnp.float32)] * 2,
        compiler_params=pltpu.CompilerParams(vmem_limit_bytes=32 * 1024 * 1024),
        name="tile_gradient",
    )(offsets, count, place, far, mid, near, probe, prop, data, table)


def around(shard, axis, by):
    count = lax.axis_size(axis)
    return lax.ppermute(shard, axis, [(i, (i + by) % count) for i in range(count)])


def partners(far, near, axis):
    count = lax.axis_size(axis)
    ends = count - 1
    outer = [(i, min(max(i + 1 if i % 2 else i - 1, 0), ends)) for i in range(count)]
    inner = [(i, i ^ 1) for i in range(count)]
    return lax.ppermute(far, axis, outer), lax.ppermute(near, axis, inner)


def on_device(
    transmission, probe_field, propagator_phase, scan_offsets, position_counts, intensities
):
    core = transmission.shape[2]
    tall, broad = lax.axis_size("ty"), lax.axis_size("tx")
    row, col = lax.axis_index("ty"), lax.axis_index("tx")
    table = jnp.asarray(dft_blocks(probe_field.shape[1]))
    prop = jnp.stack([jnp.cos(propagator_phase), jnp.sin(propagator_phase)])
    is_first = col % 2 == 0
    has_far = jnp.where(is_first, col > 0, col < broad - 1)
    place = jnp.stack([is_first, has_far]).astype(jnp.int32)
    has_above, has_below = row > 0, row < tall - 1

    def gradient(strip, far, near):
        gfar, gmid, gnear = tile_gradient(
            scan_offsets.reshape(-1), position_counts.reshape(-1), place, far, strip, near,
            probe_field, prop, intensities[0, 0], table,
        )
        far, near = partners(gfar, gnear, "tx")
        return gmid + near + jnp.where(has_far, far, 0.0)

    own = jnp.concatenate([transmission[0], transmission[1]], axis=-1)
    above = jnp.where(has_above, around(own, "ty", 1), 0.0)
    below = jnp.where(has_below, around(own, "ty", -1), 0.0)
    strip = jnp.concatenate([above, own, below], axis=1)
    for sweep in range(ITERS):
        total = gradient(strip, *partners(strip, strip, "tx"))
        top, mid, bottom = total[:, :core], total[:, core : 2 * core], total[:, 2 * core :]
        if sweep < ITERS - 1:
            down = jnp.where(has_above, around(total[:, core:], "ty", 1), 0.0)
            up = jnp.where(has_below, around(total[:, : 2 * core], "ty", -1), 0.0)
            if tall == 4:
                mixed = around(jnp.where(row < 2, bottom, top), "ty", 2)
                down2, up2 = jnp.where(row < 2, 0.0, mixed), jnp.where(row < 2, mixed, 0.0)
            else:
                down2 = jnp.where(row > 1, around(bottom, "ty", 2), 0.0)
                up2 = jnp.where(row < tall - 2, around(top, "ty", -2), 0.0)
            above = jnp.where(has_above, top + down[:, :core] + down2, 0.0)
            inside = mid + down[:, core:] + up[:, :core]
            below = jnp.where(has_below, bottom + up[:, core:] + up2, 0.0)
            strip = strip - STEP * jnp.concatenate([above, inside, below], axis=1)
        else:
            down = jnp.where(has_above, around(bottom, "ty", 1), 0.0)
            up = jnp.where(has_below, around(top, "ty", -1), 0.0)
            own = strip[:, core : 2 * core] - STEP * (mid + down + up)
    return jnp.stack([own[..., :core], own[..., core:]])


def solution(mesh):
    in_specs = (
        P(None, None, "ty", "tx"),
        P(),
        P(),
        P("ty", "tx", None, None),
        P("ty", "tx"),
        P("ty", "tx", None, None, None),
    )
    return jax.shard_map(
        on_device, mesh=mesh, in_specs=in_specs, out_specs=P(None, None, "ty", "tx"), check_vma=False
    )
```

```python
import math

import jax
import jax.numpy as jnp
import numpy as np
from jax import lax
from jax.experimental import pallas as pl
from jax.experimental.pallas import tpu as pltpu
from jax.sharding import PartitionSpec as P

ITERS = 2
STEP = 0.003
GROUP = 6


def dft_tables(length):
    half = length // 2
    inner = np.arange(half)

    def block(odd):
        order = 2 * inner + odd
        angle = 2.0 * math.pi / length * (inner[:, None] * order[None, :] % length)
        re, im = np.cos(angle) / math.sqrt(length), -np.sin(angle) / math.sqrt(length)
        return np.block([[im, re], [-re, im]]) if odd else np.block([[re, im], [-im, re]])

    tables = []
    for whole in (block(0), block(1), block(0).T, block(1).T):
        high = whole.astype(jnp.bfloat16)
        low = (whole - high.astype(np.float64)).astype(jnp.bfloat16)
        tables.append(np.block([[high, low], [high, np.zeros_like(low)]]))
    return np.stack(tables + [t.T for t in tables])


def halves(x):
    high = x.astype(jnp.bfloat16)
    return high, (x - high.astype(jnp.float32)).astype(jnp.bfloat16)


def mm(a, b):
    return jnp.dot(a, b, preferred_element_type=jnp.float32)


def gradient_kernel(
    offsets, count, place, far_ref, mid_ref, near_ref, probe_ref, prop_ref, data_ref, table_ref,
    gfar_ref, gmid_ref, gnear_ref, ext, acc,
):
    layers, rows, lanes = mid_ref.shape
    length = probe_ref.shape[1]
    core = lanes // 2
    positions = offsets.shape[0] // 2
    group = min(GROUP, positions)
    lane = lax.broadcasted_iota(jnp.int32, (rows, lanes), 1)
    low_half = lane < core
    is_first, has_far = place[0] == 1, place[1] == 1
    for s in range(layers):
        outer = jnp.where(has_far, far_ref[s], 0.0)
        left = jnp.where(is_first, outer, near_ref[s])
        right = jnp.where(is_first, near_ref[s], outer)
        mid = mid_ref[s]
        ext[s, 0, 0] = jnp.where(low_half, left, pltpu.roll(mid, core, 1))
        ext[s, 1, 0] = jnp.where(low_half, pltpu.roll(left, core, 1), mid)
        ext[s, 0, 1] = right
        ext[s, 1, 1] = pltpu.roll(right, core, 1)
    acc[...] = jnp.zeros_like(acc)

    half = length // 2
    low_lanes = lax.broadcasted_iota(jnp.int32, (length, length), 1) < half

    def swap(x):
        return pltpu.roll(x, half, 1)

    def row_products(rows, table):
        high, low = halves(jnp.concatenate(rows, axis=0))
        y = mm(jnp.concatenate([high, low], axis=1), table_ref[table])
        y = y[:, :length] + y[:, length:]
        return [y[q * length : (q + 1) * length] for q in range(len(rows))]

    def column_products(columns, table):
        high, low = halves(jnp.concatenate(columns, axis=1))
        x = jnp.concatenate([high, low], axis=0)
        y = mm(table_ref[table, :length], x) + mm(table_ref[table, length:], x)
        return [y[:, q * length : (q + 1) * length] for q in range(len(columns))]

    def rows_forward(blocks):
        evens, odds = [], []
        for re, im in blocks:
            x, y = jnp.where(low_lanes, re, im), swap(jnp.where(low_lanes, im, re))
            evens.append(x + y)
            odds.append(x - y)
        evens, odds = row_products(evens, 0), row_products(odds, 1)
        return [
            (jnp.where(low_lanes, e, o), swap(jnp.where(low_lanes, o, e)))
            for e, o in zip(evens, odds)
        ]

    def rows_inverse(blocks):
        evens, odds = [], []
        for re, im in blocks:
            turned = swap(im)
            evens.append(jnp.where(low_lanes, re, turned))
            odds.append(jnp.where(low_lanes, turned, re))
        evens, odds = row_products(evens, 2), row_products(odds, 3)
        out = []
        for e, o in zip(evens, odds):
            x, y = e + o, swap(e - o)
            out.append((jnp.where(low_lanes, x, y), jnp.where(low_lanes, y, x)))
        return out

    def columns_forward(blocks):
        evens, odds = [], []
        for re, im in blocks:
            evens.append(jnp.concatenate([re[:half] + re[half:], im[:half] + im[half:]], axis=0))
            odds.append(jnp.concatenate([re[:half] - re[half:], im[half:] - im[:half]], axis=0))
        evens, odds = column_products(evens, 4), column_products(odds, 5)
        return [
            (
                jnp.concatenate([e[:half], o[half:]], axis=0),
                jnp.concatenate([e[half:], o[:half]], axis=0),
            )
            for e, o in zip(evens, odds)
        ]

    def columns_inverse(blocks):
        evens = [jnp.concatenate([re[:half], im[:half]], axis=0) for re, im in blocks]
        odds = [jnp.concatenate([im[half:], re[half:]], axis=0) for re, im in blocks]
        evens, odds = column_products(evens, 6), column_products(odds, 7)
        return [
            (
                jnp.concatenate([e[:half] + o[:half], e[:half] - o[:half]], axis=0),
                jnp.concatenate([e[half:] - o[half:], e[half:] + o[half:]], axis=0),
            )
            for e, o in zip(evens, odds)
        ]

    def fourier(blocks):
        return columns_forward(rows_forward(blocks))

    def inverse(blocks):
        return rows_inverse(columns_inverse(blocks))

    lanes_of = lax.broadcasted_iota(jnp.int32, (length, length), 1)
    order = jnp.where(low_lanes, 2 * lanes_of, 2 * lanes_of - (length - 1))

    def even_odd(ref, k):
        rows_split = [ref[k, pl.ds(odd, half, stride=2), :] for odd in range(2)]
        return jnp.take_along_axis(jnp.concatenate(rows_split, axis=0), order, axis=1)

    def times(a, b):
        return a[0] * b[0] - a[1] * b[1], a[0] * b[1] + a[1] * b[0]

    def conj_times(a, b):
        return a[0] * b[0] + a[1] * b[1], a[0] * b[1] - a[1] * b[0]

    wide = lax.broadcasted_iota(jnp.int32, (length, lanes), 1)

    @pl.loop(0, pl.cdiv(count[0], group))
    def _(trip):
        slots = [jnp.minimum(trip * group + q, positions - 1) for q in range(group)]
        weight = [
            jnp.where(trip * group + q < count[0], 4.0, 0.0).astype(jnp.float32)
            for q in range(group)
        ]
        row = [offsets[2 * k] for k in slots]
        col = [offsets[2 * k + 1] for k in slots]

        def window(q, s):
            back = jnp.where(col[q] == 0, 0, lanes - col[q])
            parts = []
            for part in range(2):
                rows_of = pl.ds(row[q], length)
                both = jnp.where(wide >= col[q], ext[s, part, 0, rows_of, :], ext[s, part, 1, rows_of, :])
                parts.append(pltpu.roll(both, back, 1))
            return tuple(parts)

        prop = (even_odd(prop_ref, 0), even_odd(prop_ref, 1))
        probe = (probe_ref[0], probe_ref[1])
        windows = [[window(q, s) for q in range(group)] for s in range(layers)]
        fields = [[probe] * group]
        for s in range(layers):
            exits = [times(fields[s][q], windows[s][q]) for q in range(group)]
            if s < layers - 1:
                spectrum = [times(b, prop) for b in fourier(exits)]
                fields.append(inverse(spectrum))
        far = fourier(exits)
        back = []
        for q in range(group):
            re, im = far[q]
            factor = weight[q] * (re * re + im * im - even_odd(data_ref, slots[q]))
            back.append((factor * re, factor * im))
        grad = inverse(back)
        for s in reversed(range(layers)):
            for q in range(group):
                own = conj_times(fields[s][q], grad[q])
                for part in range(2):
                    turned = pltpu.roll(own[part], col[q], 1)
                    rows_of = pl.ds(row[q], length)
                    acc[s, part, 0, rows_of, :] += jnp.where(wide >= col[q], turned, 0.0)
                    acc[s, part, 1, rows_of, :] += jnp.where(wide < col[q], turned, 0.0)
            if s > 0:
                spectrum = fourier([conj_times(windows[s][q], grad[q]) for q in range(group)])
                grad = inverse([conj_times(prop, b) for b in spectrum])

    for s in range(layers):
        re0, re1, im0, im1 = acc[s, 0, 0], acc[s, 0, 1], acc[s, 1, 0], acc[s, 1, 1]
        left = jnp.where(low_half, re0, pltpu.roll(im0, core, 1))
        right = jnp.where(low_half, re1, pltpu.roll(im1, core, 1))
        gmid_ref[s] = jnp.where(low_half, pltpu.roll(re0, core, 1), im0)
        gfar_ref[s] = jnp.where(is_first, left, right)
        gnear_ref[s] = jnp.where(is_first, right, left)


def tile_gradient(offsets, count, place, far, mid, near, probe, prop, data, table):
    layers, rows, lanes = mid.shape
    vmem = pl.BlockSpec(memory_space=pltpu.VMEM)
    smem = pl.BlockSpec(memory_space=pltpu.SMEM)
    strip = jax.ShapeDtypeStruct(mid.shape, jnp.float32)
    return pl.pallas_call(
        gradient_kernel,
        out_shape=(strip, strip, strip),
        in_specs=[smem] * 3 + [vmem] * 7,
        out_specs=(vmem, vmem, vmem),
        scratch_shapes=[pltpu.VMEM((layers, 2, 2, rows, lanes), jnp.float32)] * 2,
        compiler_params=pltpu.CompilerParams(vmem_limit_bytes=32 * 1024 * 1024),
        name="tile_gradient",
    )(offsets, count, place, far, mid, near, probe, prop, data, table)


def around(shard, axis, by):
    count = lax.axis_size(axis)
    return lax.ppermute(shard, axis, [(i, (i + by) % count) for i in range(count)])


def partners(far, near, axis):
    count = lax.axis_size(axis)
    ends = count - 1
    outer = [(i, min(max(i + 1 if i % 2 else i - 1, 0), ends)) for i in range(count)]
    inner = [(i, i ^ 1) for i in range(count)]
    return lax.ppermute(far, axis, outer), lax.ppermute(near, axis, inner)


def on_device(
    transmission, probe_field, propagator_phase, scan_offsets, position_counts, intensities
):
    core = transmission.shape[2]
    tall, broad = lax.axis_size("ty"), lax.axis_size("tx")
    row, col = lax.axis_index("ty"), lax.axis_index("tx")
    table = jnp.asarray(dft_tables(probe_field.shape[1]))
    prop = jnp.stack([jnp.cos(propagator_phase), jnp.sin(propagator_phase)])
    is_first = col % 2 == 0
    has_far = jnp.where(is_first, col > 0, col < broad - 1)
    place = jnp.stack([is_first, has_far]).astype(jnp.int32)
    has_above, has_below = row > 0, row < tall - 1

    def gradient(strip, far, near):
        gfar, gmid, gnear = tile_gradient(
            scan_offsets.reshape(-1), position_counts.reshape(-1), place, far, strip, near,
            probe_field, prop, intensities[0, 0], table,
        )
        far, near = partners(gfar, gnear, "tx")
        return gmid + near + jnp.where(has_far, far, 0.0)

    own = jnp.concatenate([transmission[0], transmission[1]], axis=-1)
    above = jnp.where(has_above, around(own, "ty", 1), 0.0)
    below = jnp.where(has_below, around(own, "ty", -1), 0.0)
    strip = jnp.concatenate([above, own, below], axis=1)
    for sweep in range(ITERS):
        total = gradient(strip, *partners(strip, strip, "tx"))
        top, mid, bottom = total[:, :core], total[:, core : 2 * core], total[:, 2 * core :]
        if sweep < ITERS - 1:
            down = jnp.where(has_above, around(total[:, core:], "ty", 1), 0.0)
            up = jnp.where(has_below, around(total[:, : 2 * core], "ty", -1), 0.0)
            if tall == 4:
                mixed = around(jnp.where(row < 2, bottom, top), "ty", 2)
                down2, up2 = jnp.where(row < 2, 0.0, mixed), jnp.where(row < 2, mixed, 0.0)
            else:
                down2 = jnp.where(row > 1, around(bottom, "ty", 2), 0.0)
                up2 = jnp.where(row < tall - 2, around(top, "ty", -2), 0.0)
            above = jnp.where(has_above, top + down[:, :core] + down2, 0.0)
            inside = mid + down[:, core:] + up[:, :core]
            below = jnp.where(has_below, bottom + up[:, core:] + up2, 0.0)
            strip = strip - STEP * jnp.concatenate([above, inside, below], axis=1)
        else:
            down = jnp.where(has_above, around(bottom, "ty", 1), 0.0)
            up = jnp.where(has_below, around(top, "ty", -1), 0.0)
            own = strip[:, core : 2 * core] - STEP * (mid + down + up)
    return jnp.stack([own[..., :core], own[..., core:]])


def solution(mesh):
    in_specs = (
        P(None, None, "ty", "tx"),
        P(),
        P(),
        P("ty", "tx", None, None),
        P("ty", "tx"),
        P("ty", "tx", None, None, None),
    )
    return jax.shard_map(
        on_device, mesh=mesh, in_specs=in_specs, out_specs=P(None, None, "ty", "tx"), check_vma=False
    )
```

```python
import math

import jax
import jax.numpy as jnp
import numpy as np
from jax import lax
from jax.experimental import pallas as pl
from jax.experimental.pallas import tpu as pltpu
from jax.sharding import PartitionSpec as P

ITERS = 2
STEP = 0.003
GROUP = 6


def dft_tables(length):
    half = length // 2
    inner = np.arange(half)

    def block(odd):
        order = 2 * inner + odd
        angle = 2.0 * math.pi / length * (inner[:, None] * order[None, :] % length)
        re, im = np.cos(angle) / math.sqrt(length), -np.sin(angle) / math.sqrt(length)
        return np.block([[im, re], [-re, im]]) if odd else np.block([[re, im], [-im, re]])

    tables = []
    for whole in (block(0), block(1), block(0).T, block(1).T):
        high = whole.astype(jnp.bfloat16)
        low = (whole - high.astype(np.float64)).astype(jnp.bfloat16)
        tables.append(np.block([[high, low], [high, np.zeros_like(low)]]))
    return np.stack(tables + [t.T for t in tables])


def halves(x):
    high = x.astype(jnp.bfloat16)
    return high, (x - high.astype(jnp.float32)).astype(jnp.bfloat16)


def mm(a, b):
    return jnp.dot(a, b, preferred_element_type=jnp.float32)


def gradient_kernel(
    offsets, count, place, far_ref, mid_ref, near_ref, probe_ref, prop_ref, data_ref, table_ref,
    gfar_ref, gmid_ref, gnear_ref, ext, acc,
):
    layers, rows, lanes = mid_ref.shape
    length = probe_ref.shape[1]
    core = lanes // 2
    positions = offsets.shape[0] // 2
    group = min(GROUP, positions)
    lane = lax.broadcasted_iota(jnp.int32, (rows, lanes), 1)
    low_half = lane < core
    is_first, has_far = place[0] == 1, place[1] == 1
    for s in range(layers):
        outer = jnp.where(has_far, far_ref[s], 0.0)
        left = jnp.where(is_first, outer, near_ref[s])
        right = jnp.where(is_first, near_ref[s], outer)
        mid = mid_ref[s]
        ext[s, 0, 0] = jnp.where(low_half, left, pltpu.roll(mid, core, 1))
        ext[s, 1, 0] = jnp.where(low_half, pltpu.roll(left, core, 1), mid)
        ext[s, 0, 1] = right
        ext[s, 1, 1] = pltpu.roll(right, core, 1)
    acc[...] = jnp.zeros_like(acc)

    half = length // 2
    low_lanes = lax.broadcasted_iota(jnp.int32, (length, length), 1) < half

    def swap(x):
        return pltpu.roll(x, half, 1)

    def row_products(rows, table):
        high, low = halves(jnp.concatenate(rows, axis=0))
        y = mm(jnp.concatenate([high, low], axis=1), table_ref[table])
        y = y[:, :length] + y[:, length:]
        return [y[q * length : (q + 1) * length] for q in range(len(rows))]

    def column_products(columns, table):
        high, low = halves(jnp.concatenate(columns, axis=1))
        x = jnp.concatenate([high, low], axis=0)
        y = mm(table_ref[table], x)
        y = y[:length] + y[length:]
        return [y[:, q * length : (q + 1) * length] for q in range(len(columns))]

    def rows_forward(blocks):
        evens, odds = [], []
        for re, im in blocks:
            x, y = jnp.where(low_lanes, re, im), swap(jnp.where(low_lanes, im, re))
            evens.append(x + y)
            odds.append(x - y)
        evens, odds = row_products(evens, 0), row_products(odds, 1)
        return [
            (jnp.where(low_lanes, e, o), swap(jnp.where(low_lanes, o, e)))
            for e, o in zip(evens, odds)
        ]

    def rows_inverse(blocks):
        evens, odds = [], []
        for re, im in blocks:
            turned = swap(im)
            evens.append(jnp.where(low_lanes, re, turned))
            odds.append(jnp.where(low_lanes, turned, re))
        evens, odds = row_products(evens, 2), row_products(odds, 3)
        out = []
        for e, o in zip(evens, odds):
            x, y = e + o, swap(e - o)
            out.append((jnp.where(low_lanes, x, y), jnp.where(low_lanes, y, x)))
        return out

    def columns_forward(blocks):
        evens, odds = [], []
        for re, im in blocks:
            evens.append(jnp.concatenate([re[:half] + re[half:], im[:half] + im[half:]], axis=0))
            odds.append(jnp.concatenate([re[:half] - re[half:], im[half:] - im[:half]], axis=0))
        evens, odds = column_products(evens, 4), column_products(odds, 5)
        return [
            (
                jnp.concatenate([e[:half], o[half:]], axis=0),
                jnp.concatenate([e[half:], o[:half]], axis=0),
            )
            for e, o in zip(evens, odds)
        ]

    def columns_inverse(blocks):
        evens = [jnp.concatenate([re[:half], im[:half]], axis=0) for re, im in blocks]
        odds = [jnp.concatenate([im[half:], re[half:]], axis=0) for re, im in blocks]
        evens, odds = column_products(evens, 6), column_products(odds, 7)
        return [
            (
                jnp.concatenate([e[:half] + o[:half], e[:half] - o[:half]], axis=0),
                jnp.concatenate([e[half:] - o[half:], e[half:] + o[half:]], axis=0),
            )
            for e, o in zip(evens, odds)
        ]

    def fourier(blocks):
        return columns_forward(rows_forward(blocks))

    def inverse(blocks):
        return rows_inverse(columns_inverse(blocks))

    lanes_of = lax.broadcasted_iota(jnp.int32, (length, length), 1)
    order = jnp.where(low_lanes, 2 * lanes_of, 2 * lanes_of - (length - 1))

    def even_odd(ref, k):
        rows_split = [ref[k, pl.ds(odd, half, stride=2), :] for odd in range(2)]
        return jnp.take_along_axis(jnp.concatenate(rows_split, axis=0), order, axis=1)

    def times(a, b):
        return a[0] * b[0] - a[1] * b[1], a[0] * b[1] + a[1] * b[0]

    def conj_times(a, b):
        return a[0] * b[0] + a[1] * b[1], a[0] * b[1] - a[1] * b[0]

    wide = lax.broadcasted_iota(jnp.int32, (length, lanes), 1)

    @pl.loop(0, pl.cdiv(count[0], group))
    def _(trip):
        slots = [jnp.minimum(trip * group + q, positions - 1) for q in range(group)]
        weight = [
            jnp.where(trip * group + q < count[0], 4.0, 0.0).astype(jnp.float32)
            for q in range(group)
        ]
        row = [offsets[2 * k] for k in slots]
        col = [offsets[2 * k + 1] for k in slots]

        def window(q, s):
            back = jnp.where(col[q] == 0, 0, lanes - col[q])
            parts = []
            for part in range(2):
                rows_of = pl.ds(row[q], length)
                both = jnp.where(wide >= col[q], ext[s, part, 0, rows_of, :], ext[s, part, 1, rows_of, :])
                parts.append(pltpu.roll(both, back, 1))
            return tuple(parts)

        prop = (even_odd(prop_ref, 0), even_odd(prop_ref, 1))
        probe = (probe_ref[0], probe_ref[1])
        windows = [[window(q, s) for q in range(group)] for s in range(layers)]
        fields = [[probe] * group]
        for s in range(layers):
            exits = [times(fields[s][q], windows[s][q]) for q in range(group)]
            if s < layers - 1:
                spectrum = [times(b, prop) for b in fourier(exits)]
                fields.append(inverse(spectrum))
        far = fourier(exits)
        back = []
        for q in range(group):
            re, im = far[q]
            factor = weight[q] * (re * re + im * im - even_odd(data_ref, slots[q]))
            back.append((factor * re, factor * im))
        grad = inverse(back)
        for s in reversed(range(layers)):
            for q in range(group):
                own = conj_times(fields[s][q], grad[q])
                for part in range(2):
                    turned = pltpu.roll(own[part], col[q], 1)
                    rows_of = pl.ds(row[q], length)
                    acc[s, part, 0, rows_of, :] += jnp.where(wide >= col[q], turned, 0.0)
                    acc[s, part, 1, rows_of, :] += jnp.where(wide < col[q], turned, 0.0)
            if s > 0:
                spectrum = fourier([conj_times(windows[s][q], grad[q]) for q in range(group)])
                grad = inverse([conj_times(prop, b) for b in spectrum])

    for s in range(layers):
        re0, re1, im0, im1 = acc[s, 0, 0], acc[s, 0, 1], acc[s, 1, 0], acc[s, 1, 1]
        left = jnp.where(low_half, re0, pltpu.roll(im0, core, 1))
        right = jnp.where(low_half, re1, pltpu.roll(im1, core, 1))
        gmid_ref[s] = jnp.where(low_half, pltpu.roll(re0, core, 1), im0)
        gfar_ref[s] = jnp.where(is_first, left, right)
        gnear_ref[s] = jnp.where(is_first, right, left)


def tile_gradient(offsets, count, place, far, mid, near, probe, prop, data, table):
    layers, rows, lanes = mid.shape
    vmem = pl.BlockSpec(memory_space=pltpu.VMEM)
    smem = pl.BlockSpec(memory_space=pltpu.SMEM)
    strip = jax.ShapeDtypeStruct(mid.shape, jnp.float32)
    return pl.pallas_call(
        gradient_kernel,
        out_shape=(strip, strip, strip),
        in_specs=[smem] * 3 + [vmem] * 7,
        out_specs=(vmem, vmem, vmem),
        scratch_shapes=[pltpu.VMEM((layers, 2, 2, rows, lanes), jnp.float32)] * 2,
        compiler_params=pltpu.CompilerParams(vmem_limit_bytes=32 * 1024 * 1024),
        name="tile_gradient",
    )(offsets, count, place, far, mid, near, probe, prop, data, table)


def exchange(shard, partner):
    tall, broad = lax.axis_size("ty"), lax.axis_size("tx")
    pairs = []
    for row in range(tall):
        for col in range(broad):
            to_row, to_col = partner(row, col)
            pairs.append((row * broad + col, to_row % tall * broad + to_col % broad))
    return lax.ppermute(shard, ("ty", "tx"), pairs)


def same_chip(row, col):
    return row, col ^ 1


def other_chip(rows):
    def partner(row, col):
        broad = lax.axis_size("tx")
        to_col = col + 1 if col % 2 else col - 1
        inside = 0 <= to_col < broad
        if inside:
            return rows(row), to_col
        return (row ^ 1 if rows is same_row else rows(row)), col

    return partner


def same_row(row):
    return row


def row_pair(row):
    return row ^ 1


def row_cross(row):
    return row + 1 if row % 2 else row - 1


def two_pair(row):
    return row ^ 2


def two_cross(row):
    return row - 2 if row % 4 < 2 else row + 2


def within_column(rows):
    return lambda row, col: (rows(row), col)


def on_device(
    transmission, probe_field, propagator_phase, scan_offsets, position_counts, intensities
):
    core = transmission.shape[2]
    tall, broad = lax.axis_size("ty"), lax.axis_size("tx")
    if tall % 2 or broad % 2 or (tall > 2 and tall % 4):
        raise ValueError("unsupported mesh")
    row, col = lax.axis_index("ty"), lax.axis_index("tx")
    table = jnp.asarray(dft_tables(probe_field.shape[1]))
    prop = jnp.stack([jnp.cos(propagator_phase), jnp.sin(propagator_phase)])
    is_first = col % 2 == 0
    has_far = jnp.where(is_first, col > 0, col < broad - 1)
    place = jnp.stack([is_first, has_far]).astype(jnp.int32)
    has_above, has_below = row > 0, row < tall - 1
    odd = row % 2 == 1

    def masked(keep, x):
        return jnp.where(keep, x, 0.0)

    def sorted_rows(pair, cross):
        above = masked(has_above, jnp.where(odd, pair, cross))
        below = masked(has_below, jnp.where(odd, cross, pair))
        return above, below

    def gradient(strip, far, near):
        return tile_gradient(
            scan_offsets.reshape(-1), position_counts.reshape(-1), place, far, strip, near,
            probe_field, prop, intensities[0, 0], table,
        )

    def column_exchange(far, near):
        return exchange(far, other_chip(same_row)), exchange(near, same_chip)

    own = jnp.concatenate([transmission[0], transmission[1]], axis=-1)
    above, below = sorted_rows(
        exchange(own, within_column(row_pair)), exchange(own, within_column(row_cross))
    )
    strip = jnp.concatenate([above, own, below], axis=1)
    near = exchange(strip, same_chip)
    far_above, far_below = sorted_rows(
        exchange(own, other_chip(row_pair)), exchange(own, other_chip(row_cross))
    )
    far = jnp.concatenate([far_above, exchange(own, other_chip(same_row)), far_below], axis=1)

    for sweep in range(ITERS):
        gfar, gmid, gnear = gradient(strip, far, near)
        if sweep < ITERS - 1:
            far, near = column_exchange(gfar, gnear)
            total = gmid + near + masked(has_far, far)
            top, mid, bottom = total[:, :core], total[:, core : 2 * core], total[:, 2 * core :]
            upper, lower = total[:, : 2 * core], total[:, core:]
            pair = exchange(jnp.where(odd, upper, lower), within_column(row_pair))
            cross = exchange(jnp.where(odd, lower, upper), within_column(row_cross))
            down, up = sorted_rows(pair, cross)
            above, inside, below = top + down[:, :core], mid + down[:, core:] + up[:, :core], bottom + up[:, core:]
            if tall > 2:
                early = row % 4 < 2
                got = exchange(jnp.where(early, bottom, top), within_column(two_pair))
                above, below = above + masked(~early, got), below + masked(early, got)
            if tall > 4:
                got = exchange(jnp.where(early, top, bottom), within_column(two_cross))
                above = above + masked(early & (row > 1), got)
                below = below + masked(~early & (row < tall - 2), got)
            step = [masked(has_above, above), inside, masked(has_below, below)]
            strip = strip - STEP * jnp.concatenate(step, axis=1)
            far, near = column_exchange(strip, strip)
        else:
            total = gmid + exchange(gnear, same_chip)
            grad = total[:, core : 2 * core]
            grad += masked(has_far, exchange(gfar[:, core : 2 * core], other_chip(same_row)))
            for part, keep, reach in (
                (gfar, has_far, other_chip),
                (total, True, within_column),
            ):
                top, bottom = part[:, :core], part[:, 2 * core :]
                pair = exchange(jnp.where(odd, top, bottom), reach(row_pair))
                cross = exchange(jnp.where(odd, bottom, top), reach(row_cross))
                down, up = sorted_rows(pair, cross)
                grad += masked(keep, down + up)
            own = strip[:, core : 2 * core] - STEP * grad
    return jnp.stack([own[..., :core], own[..., core:]])


def solution(mesh):
    in_specs = (
        P(None, None, "ty", "tx"),
        P(),
        P(),
        P("ty", "tx", None, None),
        P("ty", "tx"),
        P("ty", "tx", None, None, None),
    )
    return jax.shard_map(
        on_device, mesh=mesh, in_specs=in_specs, out_specs=P(None, None, "ty", "tx"), check_vma=False
    )
```

```python
import math

import jax
import jax.numpy as jnp
import numpy as np
from jax import lax
from jax.experimental import pallas as pl
from jax.experimental.pallas import tpu as pltpu
from jax.sharding import PartitionSpec as P

ITERS = 2
STEP = 0.003
GROUP = 6


def dft_tables(length):
    half = length // 2
    inner = np.arange(half)

    def block(odd):
        order = 2 * inner + odd
        angle = 2.0 * math.pi / length * (inner[:, None] * order[None, :] % length)
        re, im = np.cos(angle) / math.sqrt(length), -np.sin(angle) / math.sqrt(length)
        return np.block([[im, re], [-re, im]]) if odd else np.block([[re, im], [-im, re]])

    tables = []
    for whole in (block(0), block(1), block(0).T, block(1).T):
        high = whole.astype(jnp.bfloat16)
        low = (whole - high.astype(np.float64)).astype(jnp.bfloat16)
        tables.append(np.block([[high, low], [high, np.zeros_like(low)]]))
    return np.stack(tables + [t.T for t in tables])


def halves(x):
    high = x.astype(jnp.bfloat16)
    return high, (x - high.astype(jnp.float32)).astype(jnp.bfloat16)


def mm(a, b):
    return jnp.dot(a, b, preferred_element_type=jnp.float32)


def column_place():
    col, broad = lax.axis_index("tx"), lax.axis_size("tx")
    is_first = lax.rem(col, 2) == 0
    return is_first, jnp.where(is_first, col, broad - 1 - col) > 0


def prepare_kernel(offsets, count, phase_ref, probe_ref, data_ref, field_ref, ordered_ref, plan_ref):
    length = phase_ref.shape[0]
    half = length // 2
    lane = lax.broadcasted_iota(jnp.int32, (length, length), 1)
    order = jnp.where(lane < half, 2 * lane, 2 * lane - (length - 1))

    def even_odd(ref):
        rows = [ref[pl.ds(odd, half, stride=2), :] for odd in range(2)]
        return jnp.take_along_axis(jnp.concatenate(rows, axis=0), order, axis=1)

    phase = even_odd(phase_ref)
    field_ref[0] = probe_ref[0]
    field_ref[1] = probe_ref[1]
    field_ref[2] = jnp.cos(phase)
    field_ref[3] = jnp.sin(phase)
    for k in range(data_ref.shape[0]):
        ordered_ref[k] = even_odd(data_ref.at[k])
    line = lax.broadcasted_iota(jnp.int32, plan_ref.shape, 0)
    slot = lax.broadcasted_iota(jnp.int32, plan_ref.shape, 1)
    plan = jnp.where(line == 2, count[0, 0], 0)
    for k in range(data_ref.shape[0]):
        pair = jnp.where(line == 0, offsets[0, k], offsets[1, k])
        plan = jnp.where((slot == k) & (line < 2), pair, plan)
    plan_ref[...] = plan


def prepared(offsets, count, phase, probe, data):
    vmem = pl.BlockSpec(memory_space=pltpu.VMEM)
    smem = pl.BlockSpec(memory_space=pltpu.SMEM)
    return pl.pallas_call(
        prepare_kernel,
        out_shape=(
            jax.ShapeDtypeStruct((4, *phase.shape), jnp.float32),
            jax.ShapeDtypeStruct(data.shape, jnp.float32),
            jax.ShapeDtypeStruct((8, 128), jnp.int32),
        ),
        in_specs=[smem] * 2 + [vmem] * 3,
        out_specs=(vmem, vmem, vmem),
        compiler_params=pltpu.CompilerParams(vmem_limit_bytes=16 * 1024 * 1024),
        name="prepare",
    )(offsets, count, phase, probe, data)


def gradient_kernel(
    plan, far_ref, mid_ref, near_ref, field_ref, data_ref, table_ref,
    gfar_ref, gmid_ref, gnear_ref, ext, acc,
):
    layers, rows, lanes = mid_ref.shape
    length = field_ref.shape[1]
    core = lanes // 2
    positions = data_ref.shape[0]
    group = min(GROUP, positions)
    lane = lax.broadcasted_iota(jnp.int32, (rows, lanes), 1)
    low_half = lane < core
    is_first, has_far = column_place()
    for s in range(layers):
        outer = jnp.where(has_far, far_ref[s], 0.0)
        left = jnp.where(is_first, outer, near_ref[s])
        right = jnp.where(is_first, near_ref[s], outer)
        mid = mid_ref[s]
        ext[s, 0, 0] = jnp.where(low_half, left, pltpu.roll(mid, core, 1))
        ext[s, 1, 0] = jnp.where(low_half, pltpu.roll(left, core, 1), mid)
        ext[s, 0, 1] = right
        ext[s, 1, 1] = pltpu.roll(right, core, 1)
    acc[...] = jnp.zeros_like(acc)

    half = length // 2
    low_lanes = lax.broadcasted_iota(jnp.int32, (length, length), 1) < half

    def swap(x):
        return pltpu.roll(x, half, 1)

    def row_products(rows, table):
        high, low = halves(jnp.concatenate(rows, axis=0))
        y = mm(jnp.concatenate([high, low], axis=1), table_ref[table])
        y = y[:, :length] + y[:, length:]
        return [y[q * length : (q + 1) * length] for q in range(len(rows))]

    def column_products(columns, table):
        high, low = halves(jnp.concatenate(columns, axis=1))
        x = jnp.concatenate([high, low], axis=0)
        y = mm(table_ref[table], x)
        y = y[:length] + y[length:]
        return [y[:, q * length : (q + 1) * length] for q in range(len(columns))]

    def rows_forward(blocks):
        evens, odds = [], []
        for re, im in blocks:
            x, y = jnp.where(low_lanes, re, im), swap(jnp.where(low_lanes, im, re))
            evens.append(x + y)
            odds.append(x - y)
        evens, odds = row_products(evens, 0), row_products(odds, 1)
        return [
            (jnp.where(low_lanes, e, o), swap(jnp.where(low_lanes, o, e)))
            for e, o in zip(evens, odds)
        ]

    def rows_inverse(blocks):
        evens, odds = [], []
        for re, im in blocks:
            turned = swap(im)
            evens.append(jnp.where(low_lanes, re, turned))
            odds.append(jnp.where(low_lanes, turned, re))
        evens, odds = row_products(evens, 2), row_products(odds, 3)
        out = []
        for e, o in zip(evens, odds):
            x, y = e + o, swap(e - o)
            out.append((jnp.where(low_lanes, x, y), jnp.where(low_lanes, y, x)))
        return out

    def columns_forward(blocks):
        evens, odds = [], []
        for re, im in blocks:
            evens.append(jnp.concatenate([re[:half] + re[half:], im[:half] + im[half:]], axis=0))
            odds.append(jnp.concatenate([re[:half] - re[half:], im[half:] - im[:half]], axis=0))
        evens, odds = column_products(evens, 4), column_products(odds, 5)
        return [
            (
                jnp.concatenate([e[:half], o[half:]], axis=0),
                jnp.concatenate([e[half:], o[:half]], axis=0),
            )
            for e, o in zip(evens, odds)
        ]

    def columns_inverse(blocks):
        evens = [jnp.concatenate([re[:half], im[:half]], axis=0) for re, im in blocks]
        odds = [jnp.concatenate([im[half:], re[half:]], axis=0) for re, im in blocks]
        evens, odds = column_products(evens, 6), column_products(odds, 7)
        return [
            (
                jnp.concatenate([e[:half] + o[:half], e[:half] - o[:half]], axis=0),
                jnp.concatenate([e[half:] - o[half:], e[half:] + o[half:]], axis=0),
            )
            for e, o in zip(evens, odds)
        ]

    def fourier(blocks):
        return columns_forward(rows_forward(blocks))

    def inverse(blocks):
        return rows_inverse(columns_inverse(blocks))

    def times(a, b):
        return a[0] * b[0] - a[1] * b[1], a[0] * b[1] + a[1] * b[0]

    def conj_times(a, b):
        return a[0] * b[0] + a[1] * b[1], a[0] * b[1] - a[1] * b[0]

    wide = lax.broadcasted_iota(jnp.int32, (length, lanes), 1)

    @pl.loop(0, pl.cdiv(plan[2, 0], group))
    def _(trip):
        slots = [jnp.minimum(trip * group + q, positions - 1) for q in range(group)]
        weight = [
            jnp.where(trip * group + q < plan[2, 0], 4.0, 0.0).astype(jnp.float32)
            for q in range(group)
        ]
        row = [plan[0, k] for k in slots]
        col = [plan[1, k] for k in slots]

        def window(q, s):
            back = jnp.where(col[q] == 0, 0, lanes - col[q])
            parts = []
            for part in range(2):
                rows_of = pl.ds(row[q], length)
                both = jnp.where(wide >= col[q], ext[s, part, 0, rows_of, :], ext[s, part, 1, rows_of, :])
                parts.append(pltpu.roll(both, back, 1))
            return tuple(parts)

        prop = (field_ref[2], field_ref[3])
        probe = (field_ref[0], field_ref[1])
        windows = [[window(q, s) for q in range(group)] for s in range(layers)]
        fields = [[probe] * group]
        for s in range(layers):
            exits = [times(fields[s][q], windows[s][q]) for q in range(group)]
            if s < layers - 1:
                spectrum = [times(b, prop) for b in fourier(exits)]
                fields.append(inverse(spectrum))
        far = fourier(exits)
        back = []
        for q in range(group):
            re, im = far[q]
            factor = weight[q] * (re * re + im * im - data_ref[slots[q]])
            back.append((factor * re, factor * im))
        grad = inverse(back)
        for s in reversed(range(layers)):
            for q in range(group):
                own = conj_times(fields[s][q], grad[q])
                for part in range(2):
                    turned = pltpu.roll(own[part], col[q], 1)
                    rows_of = pl.ds(row[q], length)
                    acc[s, part, 0, rows_of, :] += jnp.where(wide >= col[q], turned, 0.0)
                    acc[s, part, 1, rows_of, :] += jnp.where(wide < col[q], turned, 0.0)
            if s > 0:
                spectrum = fourier([conj_times(windows[s][q], grad[q]) for q in range(group)])
                grad = inverse([conj_times(prop, b) for b in spectrum])

    for s in range(layers):
        re0, re1, im0, im1 = acc[s, 0, 0], acc[s, 0, 1], acc[s, 1, 0], acc[s, 1, 1]
        left = jnp.where(low_half, re0, pltpu.roll(im0, core, 1))
        right = jnp.where(low_half, re1, pltpu.roll(im1, core, 1))
        gmid_ref[s] = jnp.where(low_half, pltpu.roll(re0, core, 1), im0)
        gfar_ref[s] = jnp.where(is_first, left, right)
        gnear_ref[s] = jnp.where(is_first, right, left)


def tile_gradient(plan, far, mid, near, field, data, table):
    layers, rows, lanes = mid.shape
    vmem = pl.BlockSpec(memory_space=pltpu.VMEM)
    smem = pl.BlockSpec(memory_space=pltpu.SMEM)
    strip = jax.ShapeDtypeStruct(mid.shape, jnp.float32)
    return pl.pallas_call(
        gradient_kernel,
        out_shape=(strip, strip, strip),
        in_specs=[smem] + [vmem] * 6,
        out_specs=(vmem, vmem, vmem),
        scratch_shapes=[pltpu.VMEM((layers, 2, 2, rows, lanes), jnp.float32)] * 2,
        compiler_params=pltpu.CompilerParams(vmem_limit_bytes=32 * 1024 * 1024),
        name="tile_gradient",
    )(plan, far, mid, near, field, data, table)


def exchange(shard, partner):
    tall, broad = lax.axis_size("ty"), lax.axis_size("tx")
    pairs = []
    for row in range(tall):
        for col in range(broad):
            to_row, to_col = partner(row, col)
            pairs.append((row * broad + col, to_row % tall * broad + to_col % broad))
    return lax.ppermute(shard, ("ty", "tx"), pairs)


def same_chip(row, col):
    return row, col ^ 1


def other_chip(rows):
    def partner(row, col):
        broad = lax.axis_size("tx")
        to_col = col + 1 if col % 2 else col - 1
        inside = 0 <= to_col < broad
        if inside:
            return rows(row), to_col
        return (row ^ 1 if rows is same_row else rows(row)), col

    return partner


def same_row(row):
    return row


def row_pair(row):
    return row ^ 1


def row_cross(row):
    return row + 1 if row % 2 else row - 1


def two_pair(row):
    return row ^ 2


def two_cross(row):
    return row - 2 if row % 4 < 2 else row + 2


def within_column(rows):
    return lambda row, col: (rows(row), col)


def on_device(
    transmission, probe_field, propagator_phase, scan_offsets, position_counts, intensities
):
    core = transmission.shape[2]
    tall, broad = lax.axis_size("ty"), lax.axis_size("tx")
    if tall % 2 or broad % 2 or (tall > 2 and tall % 4):
        raise ValueError("unsupported mesh")
    row = lax.axis_index("ty")
    table = jnp.asarray(dft_tables(probe_field.shape[1]))
    field, ordered, plan = prepared(
        scan_offsets[0, 0].T, position_counts, propagator_phase, probe_field, intensities[0, 0]
    )
    _, has_far = column_place()
    has_above, has_below = row > 0, row < tall - 1
    odd = row % 2 == 1

    def masked(keep, x):
        return jnp.where(keep, x, 0.0)

    def sorted_rows(pair, cross):
        above = masked(has_above, jnp.where(odd, pair, cross))
        below = masked(has_below, jnp.where(odd, cross, pair))
        return above, below

    def gradient(strip, far, near):
        return tile_gradient(plan, far, strip, near, field, ordered, table)

    def column_exchange(far, near):
        return (exchange(far, other_chip(same_row)), exchange(near, same_chip))

    own = jnp.concatenate([transmission[0], transmission[1]], axis=-1)
    above, below = sorted_rows(exchange(own, within_column(row_pair)), exchange(own, within_column(row_cross)))
    strip = jnp.concatenate([above, own, below], axis=1)
    near = exchange(strip, same_chip)
    far_above, far_below = sorted_rows(exchange(own, other_chip(row_pair)), exchange(own, other_chip(row_cross)))
    far = jnp.concatenate([far_above, exchange(own, other_chip(same_row)), far_below], axis=1)

    for sweep in range(ITERS):
        gfar, gmid, gnear = gradient(strip, far, near)
        if sweep < ITERS - 1:
            far, near = column_exchange(gfar, gnear)
            total = gmid + near + masked(has_far, far)
            top, mid, bottom = total[:, :core], total[:, core : 2 * core], total[:, 2 * core :]
            upper, lower = total[:, : 2 * core], total[:, core:]
            pair = exchange(jnp.where(odd, upper, lower), within_column(row_pair))
            cross = exchange(jnp.where(odd, lower, upper), within_column(row_cross))
            down, up = sorted_rows(pair, cross)
            above, inside, below = top + down[:, :core], mid + down[:, core:] + up[:, :core], bottom + up[:, core:]
            if tall > 2:
                early = row % 4 < 2
                got = exchange(jnp.where(early, bottom, top), within_column(two_pair))
                above, below = above + masked(~early, got), below + masked(early, got)
            if tall > 4:
                got = exchange(jnp.where(early, top, bottom), within_column(two_cross))
                above = above + masked(early & (row > 1), got)
                below = below + masked(~early & (row < tall - 2), got)
            step = [masked(has_above, above), inside, masked(has_below, below)]
            strip = strip - STEP * jnp.concatenate(step, axis=1)
            far, near = column_exchange(strip, strip)
        else:
            total = gmid + exchange(gnear, same_chip)
            grad = total[:, core : 2 * core]
            grad += masked(has_far, exchange(gfar[:, core : 2 * core], other_chip(same_row)))
            for part, keep, reach in ((gfar, has_far, other_chip), (total, True, within_column)):
                top, bottom = part[:, :core], part[:, 2 * core :]
                pair = exchange(jnp.where(odd, top, bottom), reach(row_pair))
                cross = exchange(jnp.where(odd, bottom, top), reach(row_cross))
                down, up = sorted_rows(pair, cross)
                grad += masked(keep, down + up)
            own = strip[:, core : 2 * core] - STEP * grad
    return jnp.stack([own[..., :core], own[..., core:]])


def solution(mesh):
    in_specs = (
        P(None, None, "ty", "tx"),
        P(),
        P(),
        P("ty", "tx", None, None),
        P("ty", "tx"),
        P("ty", "tx", None, None, None),
    )
    return jax.shard_map(
        on_device, mesh=mesh, in_specs=in_specs, out_specs=P(None, None, "ty", "tx"), check_vma=False
    )
```

```python
import math

import jax
import jax.numpy as jnp
import numpy as np
from jax import lax
from jax.experimental import pallas as pl
from jax.experimental.pallas import tpu as pltpu
from jax.sharding import PartitionSpec as P

ITERS = 2
STEP = 0.003
GROUP = 6


def dft_tables(length):
    half = length // 2
    inner = np.arange(half)

    def block(odd):
        order = 2 * inner + odd
        angle = 2.0 * math.pi / length * (inner[:, None] * order[None, :] % length)
        re, im = np.cos(angle) / math.sqrt(length), -np.sin(angle) / math.sqrt(length)
        return np.block([[im, re], [-re, im]]) if odd else np.block([[re, im], [-im, re]])

    tables = []
    for whole in (block(0), block(1), block(0).T, block(1).T):
        high = whole.astype(jnp.bfloat16)
        low = (whole - high.astype(np.float64)).astype(jnp.bfloat16)
        tables.append(np.block([[high, low], [high, np.zeros_like(low)]]))
    return np.stack(tables + [t.T for t in tables])


def halves(x):
    high = x.astype(jnp.bfloat16)
    return high, (x - high.astype(jnp.float32)).astype(jnp.bfloat16)


def mm(a, b):
    return jnp.dot(a, b, preferred_element_type=jnp.float32)


def column_place():
    col, broad = lax.axis_index("tx"), lax.axis_size("tx")
    is_first = (col & 1) == 0
    return is_first, jnp.where(is_first, col, broad - 1 - col) > 0


def prepare_kernel(offsets, count, phase_ref, probe_ref, data_ref, field_ref, ordered_ref, plan_ref):
    length = phase_ref.shape[0]
    half = length // 2
    lane = lax.broadcasted_iota(jnp.int32, (length, length), 1)
    order = jnp.where(lane < half, 2 * lane, 2 * lane - (length - 1))

    def even_odd(ref):
        rows = [ref[pl.ds(odd, half, stride=2), :] for odd in range(2)]
        return jnp.take_along_axis(jnp.concatenate(rows, axis=0), order, axis=1)

    phase = even_odd(phase_ref)
    field_ref[0] = probe_ref[0]
    field_ref[1] = probe_ref[1]
    field_ref[2] = jnp.cos(phase)
    field_ref[3] = jnp.sin(phase)
    for k in range(data_ref.shape[0]):
        ordered_ref[k] = even_odd(data_ref.at[k])
    line = lax.broadcasted_iota(jnp.int32, plan_ref.shape, 0)
    slot = lax.broadcasted_iota(jnp.int32, plan_ref.shape, 1)
    plan = jnp.where(line == 2, jnp.broadcast_to(count[...], plan_ref.shape), 0)
    for k in range(data_ref.shape[0]):
        pair = jnp.where(line == 0, offsets[0, k], offsets[1, k])
        plan = jnp.where((slot == k) & (line < 2), pair, plan)
    plan_ref[...] = plan


def prepared(offsets, count, phase, probe, data):
    vmem = pl.BlockSpec(memory_space=pltpu.VMEM)
    smem = pl.BlockSpec(memory_space=pltpu.SMEM)
    return pl.pallas_call(
        prepare_kernel,
        out_shape=(
            jax.ShapeDtypeStruct((4, *phase.shape), jnp.float32),
            jax.ShapeDtypeStruct(data.shape, jnp.float32),
            jax.ShapeDtypeStruct((8, 128), jnp.int32),
        ),
        in_specs=[smem] + [vmem] * 4,
        out_specs=(vmem, vmem, vmem),
        compiler_params=pltpu.CompilerParams(vmem_limit_bytes=16 * 1024 * 1024),
        name="prepare",
    )(offsets, count, phase, probe, data)


def gradient_kernel(
    plan, far_ref, mid_ref, near_ref, field_ref, data_ref, table_ref,
    gfar_ref, gmid_ref, gnear_ref, ext, acc,
):
    layers, rows, lanes = mid_ref.shape
    length = field_ref.shape[1]
    core = lanes // 2
    positions = data_ref.shape[0]
    group = min(GROUP, positions)
    lane = lax.broadcasted_iota(jnp.int32, (rows, lanes), 1)
    low_half = lane < core
    is_first, has_far = column_place()
    for s in range(layers):
        outer = jnp.where(has_far, far_ref[s], 0.0)
        left = jnp.where(is_first, outer, near_ref[s])
        right = jnp.where(is_first, near_ref[s], outer)
        mid = mid_ref[s]
        ext[s, 0, 0] = jnp.where(low_half, left, pltpu.roll(mid, core, 1))
        ext[s, 1, 0] = jnp.where(low_half, pltpu.roll(left, core, 1), mid)
        ext[s, 0, 1] = right
        ext[s, 1, 1] = pltpu.roll(right, core, 1)
    acc[...] = jnp.zeros_like(acc)

    half = length // 2
    low_lanes = lax.broadcasted_iota(jnp.int32, (length, length), 1) < half

    def swap(x):
        return pltpu.roll(x, half, 1)

    def row_products(rows, table):
        high, low = halves(jnp.concatenate(rows, axis=0))
        y = mm(jnp.concatenate([high, low], axis=1), table_ref[table])
        y = y[:, :length] + y[:, length:]
        return [y[q * length : (q + 1) * length] for q in range(len(rows))]

    def column_products(columns, table):
        high, low = halves(jnp.concatenate(columns, axis=1))
        x = jnp.concatenate([high, low], axis=0)
        y = mm(table_ref[table], x)
        y = y[:length] + y[length:]
        return [y[:, q * length : (q + 1) * length] for q in range(len(columns))]

    def rows_forward(blocks):
        evens, odds = [], []
        for re, im in blocks:
            x, y = jnp.where(low_lanes, re, im), swap(jnp.where(low_lanes, im, re))
            evens.append(x + y)
            odds.append(x - y)
        evens, odds = row_products(evens, 0), row_products(odds, 1)
        return [
            (jnp.where(low_lanes, e, o), swap(jnp.where(low_lanes, o, e)))
            for e, o in zip(evens, odds)
        ]

    def rows_inverse(blocks):
        evens, odds = [], []
        for re, im in blocks:
            turned = swap(im)
            evens.append(jnp.where(low_lanes, re, turned))
            odds.append(jnp.where(low_lanes, turned, re))
        evens, odds = row_products(evens, 2), row_products(odds, 3)
        out = []
        for e, o in zip(evens, odds):
            x, y = e + o, swap(e - o)
            out.append((jnp.where(low_lanes, x, y), jnp.where(low_lanes, y, x)))
        return out

    def columns_forward(blocks):
        evens, odds = [], []
        for re, im in blocks:
            evens.append(jnp.concatenate([re[:half] + re[half:], im[:half] + im[half:]], axis=0))
            odds.append(jnp.concatenate([re[:half] - re[half:], im[half:] - im[:half]], axis=0))
        evens, odds = column_products(evens, 4), column_products(odds, 5)
        return [
            (
                jnp.concatenate([e[:half], o[half:]], axis=0),
                jnp.concatenate([e[half:], o[:half]], axis=0),
            )
            for e, o in zip(evens, odds)
        ]

    def columns_inverse(blocks):
        evens = [jnp.concatenate([re[:half], im[:half]], axis=0) for re, im in blocks]
        odds = [jnp.concatenate([im[half:], re[half:]], axis=0) for re, im in blocks]
        evens, odds = column_products(evens, 6), column_products(odds, 7)
        return [
            (
                jnp.concatenate([e[:half] + o[:half], e[:half] - o[:half]], axis=0),
                jnp.concatenate([e[half:] - o[half:], e[half:] + o[half:]], axis=0),
            )
            for e, o in zip(evens, odds)
        ]

    def fourier(blocks):
        return columns_forward(rows_forward(blocks))

    def inverse(blocks):
        return rows_inverse(columns_inverse(blocks))

    def times(a, b):
        return a[0] * b[0] - a[1] * b[1], a[0] * b[1] + a[1] * b[0]

    def conj_times(a, b):
        return a[0] * b[0] + a[1] * b[1], a[0] * b[1] - a[1] * b[0]

    wide = lax.broadcasted_iota(jnp.int32, (length, lanes), 1)

    @pl.loop(0, pl.cdiv(plan[2, 0], group))
    def _(trip):
        slots = [jnp.minimum(trip * group + q, positions - 1) for q in range(group)]
        weight = [
            jnp.where(trip * group + q < plan[2, 0], 4.0, 0.0).astype(jnp.float32)
            for q in range(group)
        ]
        row = [plan[0, k] for k in slots]
        col = [plan[1, k] for k in slots]

        def window(q, s):
            rows_of = pl.ds(row[q], length)
            return tuple(
                jnp.where(wide >= col[q], ext[s, part, 0, rows_of, :], ext[s, part, 1, rows_of, :])
                for part in range(2)
            )

        prop = (field_ref[2], field_ref[3])
        probes = [
            tuple(pltpu.roll(field_ref[part], col[q], 1) for part in range(2)) for q in range(group)
        ]
        windows = [[window(q, s) for q in range(group)] for s in range(layers)]
        fields = [probes]
        for s in range(layers):
            exits = [times(fields[s][q], windows[s][q]) for q in range(group)]
            if s < layers - 1:
                spectrum = [times(b, prop) for b in fourier(exits)]
                fields.append(inverse(spectrum))
        far = fourier(exits)
        back = []
        for q in range(group):
            re, im = far[q]
            factor = weight[q] * (re * re + im * im - data_ref[slots[q]])
            back.append((factor * re, factor * im))
        grad = inverse(back)
        for s in reversed(range(layers)):
            for q in range(group):
                own = conj_times(fields[s][q], grad[q])
                for part in range(2):
                    rows_of = pl.ds(row[q], length)
                    acc[s, part, 0, rows_of, :] += jnp.where(wide >= col[q], own[part], 0.0)
                    acc[s, part, 1, rows_of, :] += jnp.where(wide < col[q], own[part], 0.0)
            if s > 0:
                spectrum = fourier([conj_times(windows[s][q], grad[q]) for q in range(group)])
                grad = inverse([conj_times(prop, b) for b in spectrum])

    for s in range(layers):
        re0, re1, im0, im1 = acc[s, 0, 0], acc[s, 0, 1], acc[s, 1, 0], acc[s, 1, 1]
        left = jnp.where(low_half, re0, pltpu.roll(im0, core, 1))
        right = jnp.where(low_half, re1, pltpu.roll(im1, core, 1))
        gmid_ref[s] = jnp.where(low_half, pltpu.roll(re0, core, 1), im0)
        gfar_ref[s] = jnp.where(is_first, left, right)
        gnear_ref[s] = jnp.where(is_first, right, left)


def tile_gradient(plan, far, mid, near, field, data, table):
    layers, rows, lanes = mid.shape
    vmem = pl.BlockSpec(memory_space=pltpu.VMEM)
    smem = pl.BlockSpec(memory_space=pltpu.SMEM)
    strip = jax.ShapeDtypeStruct(mid.shape, jnp.float32)
    return pl.pallas_call(
        gradient_kernel,
        out_shape=(strip, strip, strip),
        in_specs=[smem] + [vmem] * 6,
        out_specs=(vmem, vmem, vmem),
        scratch_shapes=[pltpu.VMEM((layers, 2, 2, rows, lanes), jnp.float32)] * 2,
        compiler_params=pltpu.CompilerParams(vmem_limit_bytes=32 * 1024 * 1024),
        name="tile_gradient",
    )(plan, far, mid, near, field, data, table)


def exchange(shard, partner):
    tall, broad = lax.axis_size("ty"), lax.axis_size("tx")
    pairs = []
    for row in range(tall):
        for col in range(broad):
            to_row, to_col = partner(row, col)
            pairs.append((row * broad + col, to_row % tall * broad + to_col % broad))
    return lax.ppermute(shard, ("ty", "tx"), pairs)


def same_chip(row, col):
    return row, col ^ 1


def other_chip(rows):
    def partner(row, col):
        broad = lax.axis_size("tx")
        to_col = col + 1 if col % 2 else col - 1
        inside = 0 <= to_col < broad
        if inside:
            return rows(row), to_col
        return (row ^ 1 if rows is same_row else rows(row)), col

    return partner


def same_row(row):
    return row


def row_pair(row):
    return row ^ 1


def row_cross(row):
    return row + 1 if row % 2 else row - 1


def two_pair(row):
    return row ^ 2


def two_cross(row):
    return row - 2 if row % 4 < 2 else row + 2


def within_column(rows):
    return lambda row, col: (rows(row), col)


def on_device(
    transmission, probe_field, propagator_phase, scan_offsets, position_counts, intensities
):
    core = transmission.shape[2]
    tall, broad = lax.axis_size("ty"), lax.axis_size("tx")
    if tall % 2 or broad % 2 or (tall > 2 and tall % 4):
        raise ValueError("unsupported mesh")
    row = lax.axis_index("ty")
    table = jnp.asarray(dft_tables(probe_field.shape[1]))
    field, ordered, plan = prepared(
        scan_offsets[0, 0].T, position_counts, propagator_phase, probe_field, intensities[0, 0]
    )
    _, has_far = column_place()
    has_above, has_below = row > 0, row < tall - 1
    odd = (row & 1) == 1

    def masked(keep, x):
        return jnp.where(keep, x, 0.0)

    def sorted_rows(pair, cross):
        above = masked(has_above, jnp.where(odd, pair, cross))
        below = masked(has_below, jnp.where(odd, cross, pair))
        return above, below

    def gradient(strip, far, near):
        return tile_gradient(plan, far, strip, near, field, ordered, table)

    def column_exchange(far, near):
        return (exchange(far, other_chip(same_row)), exchange(near, same_chip))

    own = jnp.concatenate([transmission[0], transmission[1]], axis=-1)
    above, below = sorted_rows(exchange(own, within_column(row_pair)), exchange(own, within_column(row_cross)))
    strip = jnp.concatenate([above, own, below], axis=1)
    near = exchange(strip, same_chip)
    far_above, far_below = sorted_rows(exchange(own, other_chip(row_pair)), exchange(own, other_chip(row_cross)))
    far = jnp.concatenate([far_above, exchange(own, other_chip(same_row)), far_below], axis=1)

    for sweep in range(ITERS):
        gfar, gmid, gnear = gradient(strip, far, near)
        if sweep < ITERS - 1:
            far, near = column_exchange(gfar, gnear)
            total = gmid + near + masked(has_far, far)
            top, mid, bottom = total[:, :core], total[:, core : 2 * core], total[:, 2 * core :]
            upper, lower = total[:, : 2 * core], total[:, core:]
            pair = exchange(jnp.where(odd, upper, lower), within_column(row_pair))
            cross = exchange(jnp.where(odd, lower, upper), within_column(row_cross))
            down, up = sorted_rows(pair, cross)
            above, inside, below = top + down[:, :core], mid + down[:, core:] + up[:, :core], bottom + up[:, core:]
            if tall > 2:
                early = (row & 2) == 0
                got = exchange(jnp.where(early, bottom, top), within_column(two_pair))
                above, below = above + masked(~early, got), below + masked(early, got)
            if tall > 4:
                got = exchange(jnp.where(early, top, bottom), within_column(two_cross))
                above = above + masked(early & (row > 1), got)
                below = below + masked(~early & (row < tall - 2), got)
            step = [masked(has_above, above), inside, masked(has_below, below)]
            strip = strip - STEP * jnp.concatenate(step, axis=1)
            far, near = column_exchange(strip, strip)
        else:
            total = gmid + exchange(gnear, same_chip)
            grad = total[:, core : 2 * core]
            grad += masked(has_far, exchange(gfar[:, core : 2 * core], other_chip(same_row)))
            for part, keep, reach in ((gfar, has_far, other_chip), (total, True, within_column)):
                top, bottom = part[:, :core], part[:, 2 * core :]
                pair = exchange(jnp.where(odd, top, bottom), reach(row_pair))
                cross = exchange(jnp.where(odd, bottom, top), reach(row_cross))
                down, up = sorted_rows(pair, cross)
                grad += masked(keep, down + up)
            own = strip[:, core : 2 * core] - STEP * grad
    return jnp.stack([own[..., :core], own[..., core:]])


def solution(mesh):
    in_specs = (
        P(None, None, "ty", "tx"),
        P(),
        P(),
        P("ty", "tx", None, None),
        P("ty", "tx"),
        P("ty", "tx", None, None, None),
    )
    return jax.shard_map(
        on_device, mesh=mesh, in_specs=in_specs, out_specs=P(None, None, "ty", "tx"), check_vma=False
    )
```

```python
import math

import jax
import jax.numpy as jnp
import numpy as np
from jax import lax
from jax.experimental import pallas as pl
from jax.experimental.pallas import tpu as pltpu
from jax.sharding import PartitionSpec as P

ITERS = 2
STEP = 0.003
GROUP = 6


def dft_tables(length):
    half = length // 2
    inner = np.arange(half)

    def block(odd):
        order = 2 * inner + odd
        angle = 2.0 * math.pi / length * (inner[:, None] * order[None, :] % length)
        re, im = np.cos(angle) / math.sqrt(length), -np.sin(angle) / math.sqrt(length)
        return np.block([[im, re], [-re, im]]) if odd else np.block([[re, im], [-im, re]])

    tables = []
    for whole in (block(0), block(1), block(0).T, block(1).T):
        high = whole.astype(jnp.bfloat16)
        low = (whole - high.astype(np.float64)).astype(jnp.bfloat16)
        tables.append(np.block([[high, low], [high, np.zeros_like(low)]]))
    return np.stack(tables + [t.T for t in tables])


def halves(x):
    high = x.astype(jnp.bfloat16)
    return high, (x - high.astype(jnp.float32)).astype(jnp.bfloat16)


def mm(a, b):
    return jnp.dot(a, b, preferred_element_type=jnp.float32)


def column_place():
    col, broad = lax.axis_index("tx"), lax.axis_size("tx")
    is_first = (col & 1) == 0
    return is_first, jnp.where(is_first, col, broad - 1 - col) > 0


def prepare_kernel(offsets, count, phase_ref, probe_ref, data_ref, field_ref, ordered_ref, plan_ref):
    length = phase_ref.shape[0]
    half = length // 2
    lane = lax.broadcasted_iota(jnp.int32, (length, length), 1)
    order = jnp.where(lane < half, 2 * lane, 2 * lane - (length - 1))

    def even_odd(ref):
        rows = [ref[pl.ds(odd, half, stride=2), :] for odd in range(2)]
        return jnp.take_along_axis(jnp.concatenate(rows, axis=0), order, axis=1)

    phase = even_odd(phase_ref)
    field_ref[0] = probe_ref[0]
    field_ref[1] = probe_ref[1]
    field_ref[2] = jnp.cos(phase)
    field_ref[3] = jnp.sin(phase)
    for k in range(data_ref.shape[0]):
        ordered_ref[k] = even_odd(data_ref.at[k])
    line = lax.broadcasted_iota(jnp.int32, plan_ref.shape, 0)
    slot = lax.broadcasted_iota(jnp.int32, plan_ref.shape, 1)
    plan = jnp.where(line == 2, jnp.broadcast_to(count[...], plan_ref.shape), 0)
    for k in range(data_ref.shape[0]):
        pair = jnp.where(line == 0, offsets[0, k], offsets[1, k])
        plan = jnp.where((slot == k) & (line < 2), pair, plan)
    plan_ref[...] = plan


def prepared(offsets, count, phase, probe, data):
    vmem = pl.BlockSpec(memory_space=pltpu.VMEM)
    smem = pl.BlockSpec(memory_space=pltpu.SMEM)
    return pl.pallas_call(
        prepare_kernel,
        out_shape=(
            jax.ShapeDtypeStruct((4, *phase.shape), jnp.float32),
            jax.ShapeDtypeStruct(data.shape, jnp.float32),
            jax.ShapeDtypeStruct((8, 128), jnp.int32),
        ),
        in_specs=[smem] + [vmem] * 4,
        out_specs=(vmem, vmem, vmem),
        compiler_params=pltpu.CompilerParams(vmem_limit_bytes=16 * 1024 * 1024),
        name="prepare",
    )(offsets, count, phase, probe, data)


def gradient_kernel(
    plan, far_ref, mid_ref, near_ref, field_ref, data_ref, table_ref,
    gfar_ref, gmid_ref, gnear_ref, ext, acc,
):
    layers, rows, lanes = mid_ref.shape
    length = field_ref.shape[1]
    core = lanes // 2
    positions = data_ref.shape[0]
    group = min(GROUP, positions)
    lane = lax.broadcasted_iota(jnp.int32, (rows, lanes), 1)
    low_half = lane < core
    is_first, has_far = column_place()
    for s in range(layers):
        outer = jnp.where(has_far, far_ref[s], 0.0)
        left = jnp.where(is_first, outer, near_ref[s])
        right = jnp.where(is_first, near_ref[s], outer)
        mid = mid_ref[s]
        ext[s, 0, 0] = jnp.where(low_half, left, pltpu.roll(mid, core, 1))
        ext[s, 1, 0] = jnp.where(low_half, pltpu.roll(left, core, 1), mid)
        ext[s, 0, 1] = right
        ext[s, 1, 1] = pltpu.roll(right, core, 1)
    acc[...] = jnp.zeros_like(acc)

    half = length // 2
    low_lanes = lax.broadcasted_iota(jnp.int32, (length, length), 1) < half

    def swap(x):
        return pltpu.roll(x, half, 1)

    def row_products(rows, table):
        high, low = halves(jnp.concatenate(rows, axis=0))
        y = mm(jnp.concatenate([high, low], axis=1), table_ref[table])
        y = y[:, :length] + y[:, length:]
        return [y[q * length : (q + 1) * length] for q in range(len(rows))]

    def column_products(columns, table):
        high, low = halves(jnp.concatenate(columns, axis=1))
        x = jnp.concatenate([high, low], axis=0)
        y = mm(table_ref[table], x)
        y = y[:length] + y[length:]
        return [y[:, q * length : (q + 1) * length] for q in range(len(columns))]

    def rows_forward(blocks):
        evens, odds = [], []
        for re, im in blocks:
            x, y = jnp.where(low_lanes, re, im), swap(jnp.where(low_lanes, im, re))
            evens.append(x + y)
            odds.append(x - y)
        evens, odds = row_products(evens, 0), row_products(odds, 1)
        return [
            (jnp.where(low_lanes, e, o), swap(jnp.where(low_lanes, o, e)))
            for e, o in zip(evens, odds)
        ]

    def rows_inverse(blocks):
        evens, odds = [], []
        for re, im in blocks:
            turned = swap(im)
            evens.append(jnp.where(low_lanes, re, turned))
            odds.append(jnp.where(low_lanes, turned, re))
        evens, odds = row_products(evens, 2), row_products(odds, 3)
        out = []
        for e, o in zip(evens, odds):
            x, y = e + o, swap(e - o)
            out.append((jnp.where(low_lanes, x, y), jnp.where(low_lanes, y, x)))
        return out

    def columns_forward(blocks):
        evens, odds = [], []
        for re, im in blocks:
            evens.append(jnp.concatenate([re[:half] + re[half:], im[:half] + im[half:]], axis=0))
            odds.append(jnp.concatenate([re[:half] - re[half:], im[half:] - im[:half]], axis=0))
        evens, odds = column_products(evens, 4), column_products(odds, 5)
        return [
            (
                jnp.concatenate([e[:half], o[half:]], axis=0),
                jnp.concatenate([e[half:], o[:half]], axis=0),
            )
            for e, o in zip(evens, odds)
        ]

    def columns_inverse(blocks):
        evens = [jnp.concatenate([re[:half], im[:half]], axis=0) for re, im in blocks]
        odds = [jnp.concatenate([im[half:], re[half:]], axis=0) for re, im in blocks]
        evens, odds = column_products(evens, 6), column_products(odds, 7)
        return [
            (
                jnp.concatenate([e[:half] + o[:half], e[:half] - o[:half]], axis=0),
                jnp.concatenate([e[half:] - o[half:], e[half:] + o[half:]], axis=0),
            )
            for e, o in zip(evens, odds)
        ]

    def fourier(blocks):
        return columns_forward(rows_forward(blocks))

    def inverse(blocks):
        return rows_inverse(columns_inverse(blocks))

    def times(a, b):
        return a[0] * b[0] - a[1] * b[1], a[0] * b[1] + a[1] * b[0]

    def conj_times(a, b):
        return a[0] * b[0] + a[1] * b[1], a[0] * b[1] - a[1] * b[0]

    wide = lax.broadcasted_iota(jnp.int32, (length, lanes), 1)

    @pl.loop(0, pl.cdiv(plan[2, 0], group))
    def _(trip):
        slots = [jnp.minimum(trip * group + q, positions - 1) for q in range(group)]
        weight = [
            jnp.where(trip * group + q < plan[2, 0], 4.0, 0.0).astype(jnp.float32)
            for q in range(group)
        ]
        row = [plan[0, k] for k in slots]
        col = [plan[1, k] for k in slots]

        def window(q, s):
            rows_of = pl.ds(row[q], length)
            return tuple(
                jnp.where(wide >= col[q], ext[s, part, 0, rows_of, :], ext[s, part, 1, rows_of, :])
                for part in range(2)
            )

        prop = (field_ref[2], field_ref[3])
        probes = [
            tuple(pltpu.roll(field_ref[part], col[q], 1) for part in range(2)) for q in range(group)
        ]
        windows = [[window(q, s) for q in range(group)] for s in range(layers)]
        fields = [probes]
        for s in range(layers):
            exits = [times(fields[s][q], windows[s][q]) for q in range(group)]
            if s < layers - 1:
                spectrum = [times(b, prop) for b in fourier(exits)]
                fields.append(inverse(spectrum))
        far = fourier(exits)
        back = []
        for q in range(group):
            re, im = far[q]
            factor = weight[q] * (re * re + im * im - data_ref[slots[q]])
            back.append((factor * re, factor * im))
        grad = inverse(back)
        for s in reversed(range(layers)):
            for q in range(group):
                own = conj_times(fields[s][q], grad[q])
                for part in range(2):
                    rows_of = pl.ds(row[q], length)
                    acc[s, part, 0, rows_of, :] += jnp.where(wide >= col[q], own[part], 0.0)
                    acc[s, part, 1, rows_of, :] += jnp.where(wide < col[q], own[part], 0.0)
            if s > 0:
                spectrum = fourier([conj_times(windows[s][q], grad[q]) for q in range(group)])
                grad = inverse([conj_times(prop, b) for b in spectrum])

    for s in range(layers):
        re0, re1, im0, im1 = acc[s, 0, 0], acc[s, 0, 1], acc[s, 1, 0], acc[s, 1, 1]
        left = jnp.where(low_half, re0, pltpu.roll(im0, core, 1))
        right = jnp.where(low_half, re1, pltpu.roll(im1, core, 1))
        gmid_ref[s] = jnp.where(low_half, pltpu.roll(re0, core, 1), im0)
        gfar_ref[s] = jnp.where(is_first, left, right)
        gnear_ref[s] = jnp.where(is_first, right, left)


def tile_gradient(plan, far, mid, near, field, data, table):
    layers, rows, lanes = mid.shape
    vmem = pl.BlockSpec(memory_space=pltpu.VMEM)
    smem = pl.BlockSpec(memory_space=pltpu.SMEM)
    strip = jax.ShapeDtypeStruct(mid.shape, jnp.float32)
    return pl.pallas_call(
        gradient_kernel,
        out_shape=(strip, strip, strip),
        in_specs=[smem] + [vmem] * 6,
        out_specs=(vmem, vmem, vmem),
        scratch_shapes=[pltpu.VMEM((layers, 2, 2, rows, lanes), jnp.float32)] * 2,
        compiler_params=pltpu.CompilerParams(vmem_limit_bytes=32 * 1024 * 1024),
        name="tile_gradient",
    )(plan, far, mid, near, field, data, table)


def exchange(shard, partner):
    tall, broad = lax.axis_size("ty"), lax.axis_size("tx")
    pairs = []
    for row in range(tall):
        for col in range(broad):
            to_row, to_col = partner(row, col)
            pairs.append((row * broad + col, to_row % tall * broad + to_col % broad))
    return lax.ppermute(shard, ("ty", "tx"), pairs)


def same_chip(row, col):
    return row, col ^ 1


def other_chip(rows):
    def partner(row, col):
        broad = lax.axis_size("tx")
        to_col = col + 1 if col % 2 else col - 1
        inside = 0 <= to_col < broad
        if inside:
            return (row if is_end(rows, row) else rows(row)), to_col
        return row ^ (2 if lax.axis_size("ty") > 2 else 1), col

    return partner


def is_end(rows, row):
    return rows is row_cross and row in (0, lax.axis_size("ty") - 1)


def same_row(row):
    return row


def row_pair(row):
    return row ^ 1


def row_cross(row):
    return row + 1 if row % 2 else row - 1


def two_pair(row):
    return row ^ 2


def two_cross(row):
    return row - 2 if row % 4 < 2 else row + 2


def within_column(rows):
    return lambda row, col: (row, col ^ 1) if is_end(rows, row) else (rows(row), col)


def on_device(
    transmission, probe_field, propagator_phase, scan_offsets, position_counts, intensities
):
    core = transmission.shape[2]
    tall, broad = lax.axis_size("ty"), lax.axis_size("tx")
    if tall % 2 or broad % 2 or (tall > 2 and tall % 4):
        raise ValueError("unsupported mesh")
    row = lax.axis_index("ty")
    table = jnp.asarray(dft_tables(probe_field.shape[1]))
    field, ordered, plan = prepared(
        scan_offsets[0, 0].T, position_counts, propagator_phase, probe_field, intensities[0, 0]
    )
    _, has_far = column_place()
    has_above, has_below = row > 0, row < tall - 1
    odd = (row & 1) == 1

    def masked(keep, x):
        return jnp.where(keep, x, 0.0)

    def sorted_rows(pair, cross):
        above = masked(has_above, jnp.where(odd, pair, cross))
        below = masked(has_below, jnp.where(odd, cross, pair))
        return above, below

    def gradient(strip, far, near):
        return tile_gradient(plan, far, strip, near, field, ordered, table)

    def column_exchange(far, near):
        return (exchange(far, other_chip(same_row)), exchange(near, same_chip))

    own = jnp.concatenate([transmission[0], transmission[1]], axis=-1)
    above, below = sorted_rows(exchange(own, within_column(row_pair)), exchange(own, within_column(row_cross)))
    strip = jnp.concatenate([above, own, below], axis=1)
    near = exchange(strip, same_chip)
    far_above, far_below = sorted_rows(exchange(own, other_chip(row_pair)), exchange(own, other_chip(row_cross)))
    far = jnp.concatenate([far_above, exchange(own, other_chip(same_row)), far_below], axis=1)

    for sweep in range(ITERS):
        gfar, gmid, gnear = gradient(strip, far, near)
        if sweep < ITERS - 1:
            far, near = column_exchange(gfar, gnear)
            total = gmid + near + masked(has_far, far)
            top, mid, bottom = total[:, :core], total[:, core : 2 * core], total[:, 2 * core :]
            upper, lower = total[:, : 2 * core], total[:, core:]
            pair = exchange(jnp.where(odd, upper, lower), within_column(row_pair))
            cross = exchange(jnp.where(odd, lower, upper), within_column(row_cross))
            down, up = sorted_rows(pair, cross)
            above, inside, below = top + down[:, :core], mid + down[:, core:] + up[:, :core], bottom + up[:, core:]
            if tall > 2:
                early = (row & 2) == 0
                got = exchange(jnp.where(early, bottom, top), within_column(two_pair))
                above, below = above + masked(~early, got), below + masked(early, got)
            if tall > 4:
                got = exchange(jnp.where(early, top, bottom), within_column(two_cross))
                above = above + masked(early & (row > 1), got)
                below = below + masked(~early & (row < tall - 2), got)
            step = [masked(has_above, above), inside, masked(has_below, below)]
            strip = strip - STEP * jnp.concatenate(step, axis=1)
            far, near = column_exchange(strip, strip)
        else:
            total = gmid + exchange(gnear, same_chip)
            grad = total[:, core : 2 * core]
            grad += masked(has_far, exchange(gfar[:, core : 2 * core], other_chip(same_row)))
            for part, keep, reach in ((gfar, has_far, other_chip), (total, True, within_column)):
                top, bottom = part[:, :core], part[:, 2 * core :]
                pair = exchange(jnp.where(odd, top, bottom), reach(row_pair))
                cross = exchange(jnp.where(odd, bottom, top), reach(row_cross))
                down, up = sorted_rows(pair, cross)
                grad += masked(keep, down + up)
            own = strip[:, core : 2 * core] - STEP * grad
    return jnp.stack([own[..., :core], own[..., core:]])


def solution(mesh):
    in_specs = (
        P(None, None, "ty", "tx"),
        P(),
        P(),
        P("ty", "tx", None, None),
        P("ty", "tx"),
        P("ty", "tx", None, None, None),
    )
    return jax.shard_map(
        on_device, mesh=mesh, in_specs=in_specs, out_specs=P(None, None, "ty", "tx"), check_vma=False
    )
```
